32 devices in a mesh: dom: 16 (over z, y, x), band: 2 (over core).
Axes of the slice: x: 2, y: 2, z: 4, core: 2. Of those that a mesh axis runs over, the one named last changes fastest.
Arguments:
- wavefunctions: bfloat16 [32768, 1024], P('dom', 'band'), may hold values from -4 to 4
- mass_scale: float32 [32768], P('dom'), may hold values from 0.7 to 1.4
- cell_matrices: bfloat16 [128, 512, 512], P('dom')
- connectivity: int32 [128, 512], P('dom'), may hold values from 0 to 2303, as said below
- face_index: int32 [4096], P('dom'), may hold values from 0 to 2047, as said below
Outputs:
- rotated: float32 [32768, 1024], P('dom', 'band')
The draws below stay inside these ranges and needn't reach their ends.
Inputs may be any that keep to these rules, and one draw needn't show every extreme that they name: `connectivity`: local numbers of each cell's 512 nodes within its domain: below 2048 the domain's own nodes, from 2048 on the entries of the next domain's face list in order; every local number appears in its domain, and a number may repeat. `face_index`: local numbers of 256 own nodes of each domain, in the order that the previous domain uses; a number may repeat.
All inputs are finite; a program needn't handle non-finite values.
Results may differ from the reference program's by a relative error of at most 0.011.
Values may be sent and summed in bfloat16 or wider, within the bound.
A program may use at most 64 MiB of HBM per device.

```python
import math
import jax
import jax.numpy as jnp
from jax import lax

NODE_DEV = 2048
STATES = 1024
CELL_NODES = 512
DEGREE = 3
NS_ITERS = 2
CELLS_DEV = 8
FACE = 256
NODES = 32768
CELLS = 128
FACES = 4096
N_DOM = 16


def draw_wavefunctions(key, part):
    key_one = jax.random.fold_in(jax.random.fold_in(key, 5), 0)
    values = jax.random.truncated_normal(key_one, -4.0, 4.0, (NODES, STATES), jnp.float32)
    return jnp.clip(values, -4.0, 4.0).astype(jnp.bfloat16)


def draw_cell_matrices(key, part):
    key_one, key_two = jax.random.split(jax.random.fold_in(key, 3))
    cell_shape = (CELLS, CELL_NODES, CELL_NODES)
    random_part = jax.random.normal(key_one, cell_shape, jnp.float32)
    diagonal = jax.random.uniform(key_two, (CELLS, CELL_NODES), jnp.float32, 0.5, 2.5)
    symmetric = (random_part + jnp.swapaxes(random_part, 1, 2)) / (2.0 * math.sqrt(CELL_NODES))
    identity = jnp.eye(CELL_NODES, dtype=jnp.float32)
    return (symmetric + diagonal[:, :, None] * identity[None]).astype(jnp.bfloat16)


def draw_connectivity(key, part):
    domains = CELLS // CELLS_DEV
    extent = NODE_DEV + FACE

    def one_domain(domain_key):
        key_one, key_two = jax.random.split(domain_key)
        ordering = jnp.concatenate([jax.random.permutation(key_one, extent), jax.random.permutation(key_two, extent)])
        return ordering[:CELLS_DEV * CELL_NODES].reshape(CELLS_DEV, CELL_NODES)
    domain_keys = jax.random.split(jax.random.fold_in(key, 11), domains)
    return jax.vmap(one_domain)(domain_keys).reshape(CELLS, CELL_NODES).astype(jnp.int32)


def draw_face_index(key, part):
    domains = FACES // FACE

    def one_domain(domain_key):
        chosen = jax.random.permutation(domain_key, NODE_DEV)[:FACE]
        return chosen.at[0].set(NODE_DEV - 1)
    domain_keys = jax.random.split(jax.random.fold_in(key, 17), domains)
    return jax.vmap(one_domain)(domain_keys).reshape(FACES).astype(jnp.int32)


def steps_of(rng, shape, shards, least, high):
    level = 1.0
    for dim, shards_of in shards:
        draws = jax.random.uniform(jax.random.fold_in(jax.random.fold_in(rng, 6), dim), (shards_of,), jnp.float32, least / len(shards), high / len(shards))
        level = level * jnp.repeat(jnp.exp(draws), shape[dim] // shards_of).reshape((-1,) + (1,) * (len(shape) - 1 - dim))
    return level


def setup_inputs(seed: int = 0) -> dict:
    splits = jax.random.split(jax.random.key(seed), 6)
    return {
        "wavefunctions": draw_wavefunctions(jax.random.fold_in(splits[5], 71), 0),
        "mass_scale": jnp.clip(jnp.exp(math.log(1.4) - 0.6931472 * jax.random.uniform(splits[1], (NODES,), jnp.float32) ** steps_of(splits[1], (NODES,), ((0, 16),), -0.2, 0.2)), 0.7, 1.4),
        "cell_matrices": draw_cell_matrices(jax.random.fold_in(splits[5], 71), 0),
        "connectivity": draw_connectivity(jax.random.fold_in(splits[5], 71), 0),
        "face_index": draw_face_index(jax.random.fold_in(splits[5], 71), 0),
    }


def apply_hamiltonian(vectors, mass_scale, cell_matrices, connectivity, face_index):
    band_width = vectors.shape[1]
    scaled = (mass_scale[:, None] * vectors).astype(jnp.bfloat16)
    by_domain = scaled.reshape(N_DOM, NODE_DEV, band_width)
    face_lists = face_index.reshape(N_DOM, FACE)
    face_rows = jax.vmap(lambda rows_all, picks: jnp.take(rows_all, picks, axis=0))(by_domain, face_lists)
    received = jnp.concatenate([face_rows[1:], jnp.zeros_like(face_rows[:1])], axis=0)
    extended = jnp.concatenate([by_domain, received], axis=1)
    cell_blocks = cell_matrices.reshape(N_DOM, CELLS_DEV, CELL_NODES, CELL_NODES)
    link_blocks = connectivity.reshape(N_DOM, CELLS_DEV, CELL_NODES)

    def one_domain(inputs):
        extended_rows, matrices, links = inputs
        gathered = jnp.take(extended_rows, links, axis=0).astype(jnp.float32)
        products = jnp.einsum('cij,cjs->cis', matrices.astype(jnp.float32), gathered)
        assembled = jnp.zeros((NODE_DEV + FACE, band_width), jnp.float32)
        return assembled.at[links.reshape(-1)].add(products.reshape(-1, band_width))
    assembled = lax.map(one_domain, (extended, cell_blocks, link_blocks))
    own_rows = assembled[:, :NODE_DEV]
    returned = jnp.concatenate([jnp.zeros_like(assembled[:1, NODE_DEV:]), assembled[:-1, NODE_DEV:]], axis=0)
    summed = jax.vmap(lambda target, picks, extra: target.at[picks].add(extra))(own_rows, face_lists, returned)
    return mass_scale[:, None] * summed.reshape(N_DOM * NODE_DEV, band_width)

def reference(wavefunctions, mass_scale, cell_matrices, connectivity, face_index):

    def hamiltonian(vectors):
        return apply_hamiltonian(vectors, mass_scale, cell_matrices, connectivity, face_index)
    previous = wavefunctions.astype(jnp.float32)
    current = (hamiltonian(previous) - 5.0 * previous) / 5.0
    for sweep_index in range(DEGREE - 1):
        following = 2.0 * (hamiltonian(current) - 5.0 * current) / 5.0 - previous
        previous, current = (current, following)
    filtered = current
    rounded = filtered.astype(jnp.bfloat16)
    margin = jnp.dot(rounded.T, rounded, preferred_element_type=jnp.float32) / (NODE_DEV * N_DOM)
    mean_eigen = jnp.trace(margin) / STATES
    identity = jnp.eye(STATES, dtype=jnp.float32)
    current_y = margin / mean_eigen
    current_z = identity
    highest = lax.Precision.HIGHEST
    for ns_index in range(NS_ITERS):
        product = jnp.dot(current_z, current_y, precision=highest, preferred_element_type=jnp.float32)
        correction = 1.5 * identity - 0.5 * product
        current_y = jnp.dot(current_y, correction, precision=highest, preferred_element_type=jnp.float32)
        current_z = jnp.dot(current_z, correction, precision=highest, preferred_element_type=jnp.float32)
    inverse_root = current_z / jnp.sqrt(mean_eigen)
    return jnp.dot(filtered, inverse_root, precision=highest, preferred_element_type=jnp.float32)
```

```python
import functools

import jax
import jax.numpy as jnp
from jax import lax
from jax.experimental import pallas as pl
from jax.experimental.pallas import tpu as pltpu
from jax.sharding import PartitionSpec as P

filter_center = 5.0
filter_half = 5.0
MESH = pl.DeviceIdType.MESH
VMEM_LIMIT = 62 * 1024 * 1024


def row_tile(rows, most):
    return max(t for t in range(16, most + 1, 16) if rows % t == 0)


def dot32(a, b, dims=((1,), (0,))):
    return lax.dot_general(a, b, (dims, ((), ())), preferred_element_type=jnp.float32)


def operator_kernel(share, conn_ref, a_ref, m_ref, ht, b, send_sem, recv_sem):
    cells, nodes = conn_ref.shape
    extent, width = m_ref.shape[1], b.shape[1]
    me = lax.axis_index("band") if share > 1 else 0
    if share > 1:
        barrier = pltpu.get_barrier_semaphore()
        for step in range(1, share):
            peer = lax.rem(me + step, share)
            pl.semaphore_signal(barrier, inc=1, device_id={"band": peer}, device_id_type=MESH)
        pl.semaphore_wait(barrier, share - 1)
    build = row_tile(extent, 256)

    @pl.loop(0, cells)
    def _(c):
        links = conn_ref[pl.ds(c, 1), :]
        span = pl.ds(pl.multiple_of(c * nodes, 128), nodes)

        @pl.loop(0, extent // build)
        def _(r):
            ids = lax.broadcasted_iota(jnp.int32, (build, nodes), 0) + r * build
            ht[pl.ds(pl.multiple_of(r * build, build), build), span] = jnp.where(
                ids == links, 1.0, 0.0
            ).astype(jnp.bfloat16)

    first = pl.multiple_of(me * width, 128) if share > 1 else 0

    @pl.loop(0, cells)
    def _(c):
        span = pl.ds(pl.multiple_of(c * nodes, 128), nodes)
        picks = ht[pl.ds(first, width), span]
        b[span, :] = dot32(a_ref[c], picks, ((1,), (1,))).astype(jnp.bfloat16)

    tile = row_tile(extent, 384)
    tiles = extent // tile

    def copies(r):
        rows = pl.ds(pl.multiple_of(r * tile, tile), tile)
        return [
            pltpu.make_async_remote_copy(
                src_ref=m_ref.at[me, rows],
                dst_ref=m_ref.at[me, rows],
                send_sem=send_sem.at[step, r],
                recv_sem=recv_sem.at[step, r],
                device_id={"band": lax.rem(me + step, share)},
                device_id_type=MESH,
            )
            for step in range(1, share)
        ]

    @pl.loop(0, tiles)
    def _(r):
        rows = pl.ds(pl.multiple_of(r * tile, tile), tile)
        total = dot32(ht[rows, :], b[...])
        kept = total.astype(jnp.bfloat16)
        m_ref[me, rows, :width] = kept
        offsets = lax.broadcasted_iota(jnp.int32, (tile, width), 1) - lax.broadcasted_iota(
            jnp.int32, (tile, width), 0
        )
        rest = jnp.where(
            offsets == r * tile - me * width, total - kept.astype(jnp.float32), 0.0
        )
        rest = jnp.sum(rest, axis=1, keepdims=True)
        m_ref[me, rows, width:] = jnp.broadcast_to(rest, (tile, 128)).astype(jnp.bfloat16)
        for copy in copies(r):
            copy.start()

    @pl.loop(0, tiles)
    def _(r):
        for copy in copies(r):
            copy.wait()


def domain_operator(cell_matrices, connectivity, extent):
    cells, nodes = connectivity.shape
    share = lax.axis_size("band")
    if extent % (share * 128):
        share = 1
    width = extent // share
    tiles = extent // row_tile(extent, 384)
    vmem = pl.BlockSpec(memory_space=pltpu.VMEM)
    params = dict(collective_id=0, has_side_effects=True) if share > 1 else {}
    halves = pl.pallas_call(
        functools.partial(operator_kernel, share),
        out_shape=jax.ShapeDtypeStruct((share, extent, width + 128), jnp.bfloat16),
        in_specs=[vmem] * 2,
        out_specs=vmem,
        scratch_shapes=[
            pltpu.VMEM((extent, cells * nodes), jnp.bfloat16),
            pltpu.VMEM((cells * nodes, width), jnp.bfloat16),
            pltpu.SemaphoreType.DMA((share, tiles)),
            pltpu.SemaphoreType.DMA((share, tiles)),
        ],
        compiler_params=pltpu.CompilerParams(vmem_limit_bytes=VMEM_LIMIT, **params),
        name="domain_operator",
    )(connectivity, cell_matrices)
    rest = sum(halves[i, :, width:].astype(jnp.float32) for i in range(share))
    return jnp.concatenate([halves[i, :, :width] for i in range(share)], axis=1), rest


def upper_blocks(band):
    other = 1 - band
    return (
        (2 * band, 2 * band),
        (2 * band, 2 * band + 1),
        (2 * band + 1, 2 * band + 1),
        (2 * band, 2 * other + band),
        (2 * band + 1, 2 * other + 1 - band),
    )


def split_domains(domains):
    inner = max(n for n in range(1, domains + 1) if domains % n == 0 and n * n <= domains)
    return inner, domains // inner


def margin_kernel(
    inner, outer, rounded_ref, everyone_ref, change_ref, scale_ref,
    part, first_in, first_sum, second_in, gathered, offset, second, third, term,
    band_send, band_recv, send_one, recv_one, send_two, recv_two,
    send_three, recv_three, send_four, recv_four, send_five, recv_five,
):
    rows, width = rounded_ref.shape
    states = 2 * width
    block = width // 2
    slab = block // inner
    piece = slab // outer
    chunks = 5
    me = lax.axis_index("band")
    dom = lax.axis_index("dom")
    high, low = dom // inner, lax.rem(dom, inner)
    partner = 1 - me
    plane = [high * inner + lax.rem(low + step, inner) for step in range(1, inner)]
    line = [lax.rem(high + step, outer) * inner + low for step in range(1, outer)]

    barrier = pltpu.get_barrier_semaphore()
    for peer in plane + line:
        pl.semaphore_signal(barrier, inc=1, device_id={"dom": peer}, device_id_type=MESH)
    pl.semaphore_signal(barrier, inc=1, device_id={"band": partner}, device_id_type=MESH)
    pl.semaphore_wait(barrier, inner + outer - 1)

    def remote(source, target, sends, recvs, **where):
        return pltpu.make_async_remote_copy(
            src_ref=source, dst_ref=target, send_sem=sends, recv_sem=recvs,
            device_id=where, device_id_type=MESH,
        )

    mine = pl.ds(pl.multiple_of(me * width, 128), width)
    across = remote(rounded_ref, everyone_ref.at[:, mine], band_send, band_recv, band=partner)
    across.start()
    everyone_ref[:, mine] = rounded_ref[...]

    def plane_copies(c):
        return [
            remote(
                part.at[c, pl.ds(pl.multiple_of(lax.rem(low + step, inner) * slab, slab), slab)],
                first_in.at[c, step - 1],
                send_one.at[c, step - 1], recv_one.at[c, step - 1], dom=plane[step - 1],
            )
            for step in range(1, inner)
        ]

    def line_copies(c):
        return [
            remote(
                first_sum.at[c, pl.ds(pl.multiple_of(lax.rem(high + step, outer) * piece, piece), piece)],
                second_in.at[c, step - 1],
                send_two.at[c, step - 1], recv_two.at[c, step - 1], dom=line[step - 1],
            )
            for step in range(1, outer)
        ]

    own_slab = pl.ds(pl.multiple_of(low * slab, slab), slab)
    own_piece = pl.ds(pl.multiple_of(low * slab + high * piece, piece), piece)

    def line_back(c):
        spot = gathered.at[me, c, own_piece]
        return [
            remote(spot, spot, send_three.at[c, s - 1], recv_three.at[c, s - 1], dom=line[s - 1])
            for s in range(1, outer)
        ]

    def plane_back(c):
        spot = gathered.at[me, c, own_slab]
        return [
            remote(spot, spot, send_four.at[c, s - 1], recv_four.at[c, s - 1], dom=plane[s - 1])
            for s in range(1, inner)
        ]

    def band_back(c):
        spot = gathered.at[me, c]
        return remote(spot, spot, send_five.at[c], recv_five.at[c], band=partner)

    share = 1.0 / (rows * inner * outer)

    def emit(c, left, right):
        part[c] = (dot32(left, right, ((0,), (0,))) * share).astype(jnp.bfloat16)
        for copy in plane_copies(c):
            copy.start()

    emit(0, rounded_ref[:, :block], rounded_ref[:, :block])
    emit(1, rounded_ref[:, :block], rounded_ref[:, block:])
    emit(2, rounded_ref[:, block:], rounded_ref[:, block:])
    across.wait()
    for i in range(2):
        column = partner * width + (i + me - 2 * i * me) * block
        emit(
            3 + i,
            rounded_ref[:, i * block : (i + 1) * block],
            everyone_ref[:, pl.ds(pl.multiple_of(column, 128), block)],
        )
    for c in range(chunks):
        total = part[c, own_slab].astype(jnp.float32)
        for step, copy in enumerate(plane_copies(c)):
            copy.wait()
            total = total + first_in[c, step].astype(jnp.float32)
        first_sum[c] = total.astype(jnp.bfloat16)
        for copy in line_copies(c):
            copy.start()
    for c in range(chunks):
        total = first_sum[c, pl.ds(pl.multiple_of(high * piece, piece), piece)].astype(jnp.float32)
        for step, copy in enumerate(line_copies(c)):
            copy.wait()
            total = total + second_in[c, step].astype(jnp.float32)
        gathered[me, c, own_piece] = total.astype(jnp.bfloat16)
        for copy in line_back(c):
            copy.start()
    for c in range(chunks):
        for copy in line_back(c):
            copy.wait()
        for copy in plane_back(c):
            copy.start()
    for c in range(chunks):
        for copy in plane_back(c):
            copy.wait()
        band_back(c).start()
    for c in range(chunks):
        band_back(c).wait()

    unit = (
        lax.broadcasted_iota(jnp.int32, (block, block), 0)
        == lax.broadcasted_iota(jnp.int32, (block, block), 1)
    ).astype(jnp.float32)
    trace = 0.0
    for q in range(2):
        for c in (0, 2):
            trace = trace + jnp.sum(gathered[q, c].astype(jnp.float32) * unit)
    mean_eigen = jnp.full((1, 1), trace, jnp.float32) / states
    inverse = 1.0 / mean_eigen
    scale_ref[...] = jnp.broadcast_to(lax.rsqrt(mean_eigen), scale_ref.shape)
    for q in range(2):
        for c, (i, j) in enumerate(upper_blocks(q)):
            value = gathered[q, c].astype(jnp.float32) * inverse
            if i == j:
                value = value - unit
            offset[i * block : (i + 1) * block, j * block : (j + 1) * block] = value.astype(jnp.bfloat16)
            if i != j:
                offset[j * block : (j + 1) * block, i * block : (i + 1) * block] = value.T.astype(jnp.bfloat16)

    tiles = states // block

    def span(r):
        return pl.ds(pl.multiple_of(r * block, block), block)

    @pl.loop(0, tiles)
    def _(r):
        value = dot32(offset[span(r), :], offset[:, mine])
        second[span(r), :] = value
        term[span(r), :] = value.astype(jnp.bfloat16)

    @pl.loop(0, tiles)
    def _(r):
        third[span(r), :] = (
            dot32(offset[span(r), :], term[...]) / 16.0 - second[span(r), :] * (5.0 / 16.0)
        ).astype(jnp.bfloat16)

    @pl.loop(0, tiles)
    def _(r):
        tail = dot32(offset[span(r), :], third[...])
        first = offset[span(r), mine].astype(jnp.float32)
        change_ref[span(r), :] = (tail + 0.375 * second[span(r), :] - 0.5 * first).astype(jnp.bfloat16)


def margin_root(rounded, domains):
    bf16 = jnp.bfloat16
    rows, width = rounded.shape
    states, block = 2 * width, width // 2
    inner, outer = split_domains(domains)
    slab = block // inner
    piece = slab // outer
    vmem = pl.BlockSpec(memory_space=pltpu.VMEM)
    dma = pltpu.SemaphoreType.DMA
    return pl.pallas_call(
        functools.partial(margin_kernel, inner, outer),
        out_shape=(
            jax.ShapeDtypeStruct((rows, states), bf16),
            jax.ShapeDtypeStruct((states, width), bf16),
            jax.ShapeDtypeStruct((8, 128), jnp.float32),
        ),
        in_specs=[vmem],
        out_specs=(vmem, vmem, vmem),
        scratch_shapes=[
            pltpu.VMEM((5, block, block), bf16),
            pltpu.VMEM((5, inner - 1, slab, block), bf16),
            pltpu.VMEM((5, slab, block), bf16),
            pltpu.VMEM((5, outer - 1, piece, block), bf16),
            pltpu.VMEM((2, 5, block, block), bf16),
            pltpu.VMEM((states, states), bf16),
            pltpu.VMEM((states, width), jnp.float32),
            pltpu.VMEM((states, width), bf16),
            pltpu.VMEM((states, width), bf16),
            dma, dma,
            dma((5, inner - 1)), dma((5, inner - 1)),
            dma((5, outer - 1)), dma((5, outer - 1)),
            dma((5, outer - 1)), dma((5, outer - 1)),
            dma((5, inner - 1)), dma((5, inner - 1)),
            dma((5,)), dma((5,)),
        ],
        compiler_params=pltpu.CompilerParams(
            vmem_limit_bytes=VMEM_LIMIT, collective_id=1, has_side_effects=True
        ),
        name="margin_root",
    )(rounded)


def passed_along(value, axis, steps):
    count = lax.axis_size(axis)
    initial, last = (max(0, -steps), min(count, count - steps))
    return lax.ppermute(value, axis, [(source, source + steps) for source in range(initial, last)])


def on_device(wavefunctions, mass_scale, cell_matrices, connectivity, face_index):
    bf16 = jnp.bfloat16
    own, band_width = wavefunctions.shape
    face = face_index.shape[0]
    domains = lax.axis_size("dom")
    states = band_width * lax.axis_size("band")
    matrix, rest = domain_operator(cell_matrices, connectivity, own + face)
    face_of = (face_index[:, None] == lax.broadcasted_iota(jnp.int32, (face, own), 1)).astype(bf16)
    face_in = (face_index[None, :] == lax.broadcasted_iota(jnp.int32, (own, face), 0)).astype(bf16)
    outgoing = jnp.concatenate([matrix[own:, :own], face_of], axis=0)
    inner = matrix[:own, :own]
    edge = jnp.concatenate([matrix[:own, own:], face_in, face_in], axis=1)
    corner = jnp.concatenate([matrix[own:, own:], rest[own:].astype(bf16)], axis=1)
    corner = passed_along(corner, "dom", 1)
    corner, corner_rest = corner[:, :face], corner[:, face : face + 1].astype(jnp.float32)
    rest = rest[:own, :1]
    mass = mass_scale[:, None]

    def hamiltonian(vectors):
        scaled = (mass * vectors).astype(bf16)
        sent = dot32(outgoing, scaled).astype(bf16)
        returned = passed_along(sent[:face], "dom", 1)
        received = passed_along(sent[face:], "dom", -1)
        summed = dot32(inner, scaled) + rest * scaled.astype(jnp.float32)
        added = returned.astype(jnp.float32) + dot32(corner, sent[face:])
        added = added + corner_rest * sent[face:].astype(jnp.float32)
        high = added.astype(bf16)
        low = (added - lax.reduce_precision(added, 8, 7)).astype(bf16)
        summed = summed + dot32(edge, jnp.concatenate([received, high, low], axis=0))
        return mass * summed

    previous = wavefunctions.astype(jnp.float32)
    current = (hamiltonian(previous) - filter_center * previous) / filter_half
    for _ in range(2):
        following = 2.0 * (hamiltonian(current) - filter_center * current) / filter_half - previous
        previous, current = (current, following)
    rounded = current.astype(bf16)
    if lax.axis_size("band") == 2 and min(split_domains(domains)) > 1 and band_width % (32 * domains) == 0:
        everyone, change, scale = margin_root(rounded, domains)
        return (current + dot32(everyone, change)) * scale[0, 0]
    everyone = lax.all_gather(rounded, "band", axis=1, tiled=True)
    partial = dot32(everyone, rounded, ((0,), (0,))) / (own * domains)
    tile = lax.psum_scatter(partial.astype(bf16), "dom", scatter_dimension=0, tiled=True)
    columns = lax.all_gather(tile, "dom", axis=0, tiled=True)
    margin = lax.all_gather(columns, "band", axis=1, tiled=True).astype(jnp.float32)
    identity = (
        lax.broadcasted_iota(jnp.int32, (states, states), 0)
        == lax.broadcasted_iota(jnp.int32, (states, states), 1)
    ).astype(jnp.float32)
    mean_eigen = jnp.sum(margin * identity) / states
    offset = (margin / mean_eigen - identity).astype(bf16)
    start = lax.axis_index("band") * band_width
    first = lax.dynamic_slice_in_dim(columns.astype(jnp.float32), 0, states, 0) / mean_eigen
    first = first - lax.dynamic_slice_in_dim(identity, start, band_width, 1)
    second = dot32(offset, first.astype(bf16))
    third = dot32(offset, second.astype(bf16))
    tail = dot32(offset, (third / 16.0 - second * (5.0 / 16.0)).astype(bf16))
    change = tail + 0.375 * second - 0.5 * first
    turned = current + dot32(everyone, change.astype(bf16))
    return turned / jnp.sqrt(mean_eigen)


def solution(mesh):
    return jax.shard_map(
        on_device,
        mesh=mesh,
        in_specs=(P("dom", "band"), P("dom"), P("dom", None, None), P("dom", None), P("dom")),
        out_specs=P("dom", "band"),
        check_vma=False,
    )
```

```python
import functools

import jax
import jax.numpy as jnp
from jax import lax
from jax.experimental import pallas as pl
from jax.experimental.pallas import tpu as pltpu
from jax.sharding import PartitionSpec as P

filter_center = 5.0
filter_half = 5.0
MESH = pl.DeviceIdType.MESH
VMEM_LIMIT = 62 * 1024 * 1024
FUSED_LIMIT = 67043328


def row_tile(rows, most):
    return max(t for t in range(16, most + 1, 16) if rows % t == 0)


def dot32(a, b, dims=((1,), (0,))):
    return lax.dot_general(a, b, (dims, ((), ())), preferred_element_type=jnp.float32)


def operator_kernel(share, conn_ref, a_ref, m_ref, ht, b, send_sem, recv_sem):
    cells, nodes = conn_ref.shape
    extent, width = m_ref.shape[1], b.shape[1]
    me = lax.axis_index("band") if share > 1 else 0
    if share > 1:
        barrier = pltpu.get_barrier_semaphore()
        for step in range(1, share):
            peer = lax.rem(me + step, share)
            pl.semaphore_signal(barrier, inc=1, device_id={"band": peer}, device_id_type=MESH)
        pl.semaphore_wait(barrier, share - 1)
    build = row_tile(extent, 256)

    @pl.loop(0, cells)
    def _(c):
        links = conn_ref[pl.ds(c, 1), :]
        span = pl.ds(pl.multiple_of(c * nodes, 128), nodes)

        @pl.loop(0, extent // build)
        def _(r):
            ids = lax.broadcasted_iota(jnp.int32, (build, nodes), 0) + r * build
            ht[pl.ds(pl.multiple_of(r * build, build), build), span] = jnp.where(
                ids == links, 1.0, 0.0
            ).astype(jnp.bfloat16)

    first = pl.multiple_of(me * width, 128) if share > 1 else 0

    @pl.loop(0, cells)
    def _(c):
        span = pl.ds(pl.multiple_of(c * nodes, 128), nodes)
        picks = ht[pl.ds(first, width), span]
        b[span, :] = dot32(a_ref[c], picks, ((1,), (1,))).astype(jnp.bfloat16)

    tile = row_tile(extent, 384)
    tiles = extent // tile

    def copies(r):
        rows = pl.ds(pl.multiple_of(r * tile, tile), tile)
        return [
            pltpu.make_async_remote_copy(
                src_ref=m_ref.at[me, rows],
                dst_ref=m_ref.at[me, rows],
                send_sem=send_sem.at[step, r],
                recv_sem=recv_sem.at[step, r],
                device_id={"band": lax.rem(me + step, share)},
                device_id_type=MESH,
            )
            for step in range(1, share)
        ]

    @pl.loop(0, tiles)
    def _(r):
        rows = pl.ds(pl.multiple_of(r * tile, tile), tile)
        total = dot32(ht[rows, :], b[...])
        kept = total.astype(jnp.bfloat16)
        m_ref[me, rows, :width] = kept
        offsets = lax.broadcasted_iota(jnp.int32, (tile, width), 1) - lax.broadcasted_iota(
            jnp.int32, (tile, width), 0
        )
        rest = jnp.where(
            offsets == r * tile - me * width, total - kept.astype(jnp.float32), 0.0
        )
        rest = jnp.sum(rest, axis=1, keepdims=True)
        m_ref[me, rows, width:] = jnp.broadcast_to(rest, (tile, 128)).astype(jnp.bfloat16)
        for copy in copies(r):
            copy.start()

    @pl.loop(0, tiles)
    def _(r):
        for copy in copies(r):
            copy.wait()


def domain_operator(cell_matrices, connectivity, extent):
    cells, nodes = connectivity.shape
    share = lax.axis_size("band")
    if extent % (share * 128):
        share = 1
    width = extent // share
    tiles = extent // row_tile(extent, 384)
    vmem = pl.BlockSpec(memory_space=pltpu.VMEM)
    params = dict(collective_id=0, has_side_effects=True) if share > 1 else {}
    halves = pl.pallas_call(
        functools.partial(operator_kernel, share),
        out_shape=jax.ShapeDtypeStruct((share, extent, width + 128), jnp.bfloat16),
        in_specs=[vmem] * 2,
        out_specs=vmem,
        scratch_shapes=[
            pltpu.VMEM((extent, cells * nodes), jnp.bfloat16),
            pltpu.VMEM((cells * nodes, width), jnp.bfloat16),
            pltpu.SemaphoreType.DMA((share, tiles)),
            pltpu.SemaphoreType.DMA((share, tiles)),
        ],
        compiler_params=pltpu.CompilerParams(vmem_limit_bytes=VMEM_LIMIT, **params),
        name="domain_operator",
    )(connectivity, cell_matrices)
    rest = sum(halves[i, :, width:].astype(jnp.float32) for i in range(share))
    return jnp.concatenate([halves[i, :, :width] for i in range(share)], axis=1), rest


def upper_blocks(band):
    other = 1 - band
    return (
        (2 * band, 2 * band),
        (2 * band, 2 * band + 1),
        (2 * band + 1, 2 * band + 1),
        (2 * band, 2 * other + band),
        (2 * band + 1, 2 * other + 1 - band),
    )


def split_domains(domains):
    inner = max(n for n in range(1, domains + 1) if domains % n == 0 and n * n <= domains)
    return inner, domains // inner


def column_form(row):
    return jnp.broadcast_to(row, (128, 128)).T


def one_hot(ids, links):
    return jnp.where(ids == links, 1.0, 0.0).astype(jnp.bfloat16)


def span(index, size):
    return pl.ds(pl.multiple_of(index * size, size), size)


def fused_kernel(inner, outer, names, *args):
    refs = dict(zip(names, args))
    conn_ref, a_ref, mass_ref, face_ref, wave_ref = (refs[n] for n in names[:5])
    everyone_out, filtered_out, change_ref, scale_ref = (refs[n] for n in names[5:9])
    matrix, b, picks, hits = (refs[n] for n in ("matrix", "b", "picks", "hits"))
    mass_all, face_column, face_of, face_in = (
        refs[n] for n in ("mass_all", "face_column", "face_of", "face_in")
    )
    scaled, sent, returned_in, faces_in, corner_in = (
        refs[n] for n in ("scaled", "sent", "returned_in", "faces_in", "corner_in")
    )
    rests, rest_all, corner_rest, corner_rest_in, added_low = (
        refs[n] for n in ("rests", "rest_all", "corner_rest", "corner_rest_in", "added_low")
    )
    states_one, states_two, everyone = (refs[n] for n in ("states_one", "states_two", "everyone"))
    part, first_in, first_sum, second_in, gathered = (
        refs[n] for n in ("part", "first_in", "first_sum", "second_in", "gathered")
    )
    offset, second, third, term = (refs[n] for n in ("offset", "second", "third", "term"))
    bf16, f32 = jnp.bfloat16, jnp.float32
    cells, nodes = conn_ref.shape
    own, width = wave_ref.shape
    face = face_ref.shape[1]
    extent = own + face
    states, block = 2 * width, width // 2
    share = extent // 2
    domains = inner * outer
    slab, piece = block // inner, block // inner // outer
    chunks = 5
    me = lax.axis_index("band")
    dom = lax.axis_index("dom")
    high, low = dom // inner, lax.rem(dom, inner)
    partner = 1 - me
    after, before = lax.rem(dom + 1, domains), lax.rem(dom + domains - 1, domains)
    plane = [high * inner + lax.rem(low + step, inner) for step in range(1, inner)]
    line = [lax.rem(high + step, outer) * inner + low for step in range(1, outer)]
    has_after, has_before = dom < domains - 1, dom > 0

    barrier = pltpu.get_barrier_semaphore()
    for peer in plane + line + [after, before]:
        pl.semaphore_signal(barrier, inc=1, device_id={"dom": peer}, device_id_type=MESH)
    pl.semaphore_signal(barrier, inc=1, device_id={"band": partner}, device_id_type=MESH)

    def remote(source, target, name, *at, **where):
        return pltpu.make_async_remote_copy(
            src_ref=source, dst_ref=target,
            send_sem=refs[name + "_send"].at[at], recv_sem=refs[name + "_recv"].at[at],
            device_id=where, device_id_type=MESH,
        )

    @pl.loop(0, own // 128)
    def _(i):
        mass_all[span(i, 128), :] = column_form(mass_ref[:, span(i, 128)])

    for i in range(face // 128):
        face_column[i * 128 : (i + 1) * 128, :] = column_form(
            face_ref[:, i * 128 : (i + 1) * 128].astype(f32)
        ).astype(jnp.int32)

    @pl.loop(0, own // 128)
    def _(i):
        ids = lax.broadcasted_iota(jnp.int32, (face, 128), 1) + i * 128
        face_of[:, span(i, 128)] = one_hot(ids, face_column[...])
        ids = lax.broadcasted_iota(jnp.int32, (128, face), 0) + i * 128
        face_in[span(i, 128), :] = one_hot(ids, face_ref[...])

    def wide(value):
        return jnp.concatenate([value] * (block // 128), axis=1)

    def mass_tile(rows):
        return wide(mass_all[rows, :])

    @pl.loop(0, own // face)
    def _(t):
        rows = span(t, face)
        for h in range(2):
            value = wave_ref[rows, h * block : (h + 1) * block].astype(f32)
            scaled[h, rows, :] = (mass_tile(rows) * value).astype(bf16)

    for k in range(3):
        for h in range(2):
            @pl.when(jnp.logical_not(has_after))
            def _():
                faces_in[k, h] = jnp.zeros_like(faces_in[k, h])

            @pl.when(jnp.logical_not(has_before))
            def _():
                returned_in[k, h] = jnp.zeros_like(returned_in[k, h])

    @pl.when(jnp.logical_not(has_before))
    def _():
        corner_in[...] = jnp.zeros_like(corner_in)
        corner_rest_in[...] = jnp.zeros_like(corner_rest_in)

    def face_copy(k, h):
        return remote(sent.at[k, h, pl.ds(face, face)], faces_in.at[k, h], "face", k, h, dom=before)

    def return_copy(k, h):
        return remote(sent.at[k, h, pl.ds(0, face)], returned_in.at[k, h], "return", k, h, dom=after)

    def corner_copy():
        source = matrix.at[pl.ds(own, face), pl.ds(own, face)]
        return remote(source, corner_in, "corner", 0, dom=after)

    def corner_rest_copy():
        return remote(corner_rest, corner_rest_in, "corner", 1, dom=after)

    def send_faces(k, h):
        sent[k, h, face:] = dot32(face_of[...], scaled[h]).astype(bf16)

        @pl.when(has_before)
        def _():
            face_copy(k, h).start()

    def send_returned(k, h):
        sent[k, h, :face] = dot32(matrix[own:, :own], scaled[h]).astype(bf16)

        @pl.when(has_after)
        def _():
            return_copy(k, h).start()

    pl.semaphore_wait(barrier, inner + outer + 1)
    for h in range(2):
        send_faces(0, h)

    columns = pl.ds(pl.multiple_of(me * share, 128), share)

    @pl.loop(0, cells)
    def _(c):
        links = conn_ref[pl.ds(c, 1), :]

        @pl.loop(0, share // 128)
        def _(r):
            ids = lax.broadcasted_iota(jnp.int32, (128, nodes), 0) + (r * 128 + me * share)
            picks[span(r, 128), :] = one_hot(ids, links)

        b[span(c, nodes), :] = dot32(a_ref[c], picks[...], ((1,), (1,))).astype(bf16)

    tiles = extent // face

    def matrix_copy(r):
        spot = matrix.at[span(tiles - 1 - r, face), columns]
        return remote(spot, spot, "matrix", r, band=partner)

    def rest_copy(r):
        spot = rests.at[me, span(tiles - 1 - r, face)]
        return remote(spot, spot, "rest", r, band=partner)

    @pl.loop(0, tiles)
    def _(r):
        t = tiles - 1 - r
        for c in range(cells):
            ids = lax.broadcasted_iota(jnp.int32, (face, nodes), 0) + t * face
            hits[:, c * nodes : (c + 1) * nodes] = one_hot(ids, conn_ref[c : c + 1, :])
        total = dot32(hits[...], b[...])
        kept = total.astype(bf16)
        matrix[span(t, face), columns] = kept
        gaps = lax.broadcasted_iota(jnp.int32, (face, share), 1) - lax.broadcasted_iota(
            jnp.int32, (face, share), 0
        )
        rest = jnp.where(gaps == t * face - me * share, total - kept.astype(f32), 0.0)
        rest = jnp.sum(rest, axis=1, keepdims=True)
        rests[me, span(t, face), :] = jnp.broadcast_to(rest, (face, 128)).astype(bf16)
        matrix_copy(r).start()
        rest_copy(r).start()

        @pl.when(r == 1)
        def _():
            matrix_copy(0).wait()
            rest_copy(0).wait()
            corner_rest[...] = rests[0, own:, :] + rests[1, own:, :]

            @pl.when(has_after)
            def _():
                corner_copy().start()
                corner_rest_copy().start()

            for h in range(2):
                send_returned(0, h)

    @pl.loop(1, tiles)
    def _(r):
        matrix_copy(r).wait()
        rest_copy(r).wait()

    @pl.loop(0, own // face)
    def _(t):
        rows = span(t, face)
        rest_all[rows, :] = rests[0, rows, :].astype(f32) + rests[1, rows, :].astype(f32)

    ratio = 1.0 / filter_half
    shift = filter_center / filter_half

    def wave_tile(h, rows):
        return wave_ref[rows, h * block : (h + 1) * block].astype(f32)

    def advance(k, h):
        target = states_two if k == 1 else states_one

        @pl.loop(0, own // face)
        def _(t):
            rows = span(t, face)
            value = dot32(matrix[rows, :own], scaled[h])
            value = value + wide(rest_all[rows, :]) * scaled[h, rows, :].astype(f32)
            value = value * mass_tile(rows)
            if k == 0:
                target[h, rows, :] = ratio * value - shift * wave_tile(h, rows)
            elif k == 1:
                target[h, rows, :] = (
                    2.0 * ratio * value - 2.0 * shift * states_one[h, rows, :] - wave_tile(h, rows)
                )
            else:
                target[h, rows, :] = (
                    2.0 * ratio * value - 2.0 * shift * states_two[h, rows, :] - states_one[h, rows, :]
                )

        def wait_both(copies):
            for copy, sends, receives in copies:
                @pl.when(sends)
                def _():
                    copy.wait_send()

                @pl.when(receives)
                def _():
                    copy.wait_recv()

        waits = [(face_copy(k, h), has_before, has_after), (return_copy(k, h), has_after, has_before)]
        if k == 0 and h == 0:
            waits.append((corner_copy(), has_after, has_before))
            waits.append((corner_rest_copy(), has_after, has_before))
        wait_both(waits)
        added = returned_in[k, h].astype(f32) + dot32(corner_in[...], sent[k, h, face:])
        added = added + wide(corner_rest_in[...].astype(f32)) * sent[k, h, face:].astype(f32)
        kept = added.astype(bf16)
        sent[k, h, :face] = kept
        added_low[...] = (added - kept.astype(f32)).astype(bf16)
        scale = ratio if k == 0 else 2.0 * ratio

        @pl.loop(0, own // face)
        def _(t):
            rows = span(t, face)
            value = dot32(matrix[rows, own:], faces_in[k, h]) + dot32(face_in[rows, :], sent[k, h, :face])
            value = value + dot32(face_in[rows, :], added_low[...])
            mass = mass_tile(rows)
            value = target[h, rows, :] + scale * value * mass
            target[h, rows, :] = value
            if k < 2:
                scaled[h, rows, :] = (mass * value).astype(bf16)
            else:
                everyone[2 * me + h, rows, :] = value.astype(bf16)

    def band_copy(h):
        spot = everyone.at[2 * me + h]
        return remote(spot, spot, "band", h, band=partner)

    def local(source, target, index):
        return pltpu.make_async_copy(source, target, refs["local_sem"].at[index])

    def filtered_copy(h):
        return local(states_one.at[h], filtered_out.at[h], h)

    def everyone_copy(i):
        q = 2 * me + i if i < 2 else 2 * partner + i - 2
        return local(everyone.at[q], everyone_out.at[q], 2 + i)

    def plane_copies(c):
        return [
            remote(
                part.at[c, span(lax.rem(low + step, inner), slab)],
                first_in.at[c, step - 1], "one", c, step - 1, dom=plane[step - 1],
            )
            for step in range(1, inner)
        ]

    def line_copies(c):
        return [
            remote(
                first_sum.at[c, span(lax.rem(high + step, outer), piece)],
                second_in.at[c, step - 1], "two", c, step - 1, dom=line[step - 1],
            )
            for step in range(1, outer)
        ]

    own_slab = span(low, slab)
    own_piece = pl.ds(pl.multiple_of(low * slab + high * piece, piece), piece)

    def line_back(c):
        spot = gathered.at[me, c, own_piece]
        return [remote(spot, spot, "three", c, s - 1, dom=line[s - 1]) for s in range(1, outer)]

    def plane_back(c):
        spot = gathered.at[me, c, own_slab]
        return [remote(spot, spot, "four", c, s - 1, dom=plane[s - 1]) for s in range(1, inner)]

    def band_back(c):
        spot = gathered.at[me, c]
        return remote(spot, spot, "five", c, band=partner)

    def emit(c, left, right):
        value = dot32(everyone[left], everyone[right], ((0,), (0,)))
        part[c] = (value * (1.0 / (own * domains))).astype(bf16)
        for copy in plane_copies(c):
            copy.start()

    for k in range(3):
        for h in range(2):
            advance(k, h)
            if k < 2:
                send_faces(k + 1, h)
                send_returned(k + 1, h)
            else:
                band_copy(h).start()
                filtered_copy(h).start()
                everyone_copy(h).start()
                if h == 0:
                    emit(0, 2 * me, 2 * me)
    emit(1, 2 * me, 2 * me + 1)
    emit(2, 2 * me + 1, 2 * me + 1)
    for h in range(2):
        band_copy(h).wait()
        everyone_copy(2 + h).start()
    for i in range(2):
        emit(3 + i, 2 * me + i, 2 * partner + i + me - 2 * i * me)

    for c in range(chunks):
        total = part[c, own_slab].astype(f32)
        for step, copy in enumerate(plane_copies(c)):
            copy.wait()
            total = total + first_in[c, step].astype(f32)
        first_sum[c] = total.astype(bf16)
        for copy in line_copies(c):
            copy.start()
    for c in range(chunks):
        total = first_sum[c, span(high, piece)].astype(f32)
        for step, copy in enumerate(line_copies(c)):
            copy.wait()
            total = total + second_in[c, step].astype(f32)
        gathered[me, c, own_piece] = total.astype(bf16)
        for copy in line_back(c):
            copy.start()
    for c in range(chunks):
        for copy in line_back(c):
            copy.wait()
        for copy in plane_back(c):
            copy.start()
    for c in range(chunks):
        for copy in plane_back(c):
            copy.wait()
        band_back(c).start()
    for c in range(chunks):
        band_back(c).wait()

    unit = (
        lax.broadcasted_iota(jnp.int32, (block, block), 0)
        == lax.broadcasted_iota(jnp.int32, (block, block), 1)
    ).astype(f32)
    trace = 0.0
    for q in range(2):
        for c in (0, 2):
            trace = trace + jnp.sum(gathered[q, c].astype(f32) * unit)
    mean_eigen = jnp.full((1, 1), trace, f32) / states
    inverse = 1.0 / mean_eigen
    scale_ref[...] = jnp.broadcast_to(lax.rsqrt(mean_eigen), scale_ref.shape)
    for q in range(2):
        for c, (i, j) in enumerate(upper_blocks(q)):
            value = gathered[q, c].astype(f32) * inverse
            if i == j:
                value = value - unit
            offset[i * block : (i + 1) * block, j * block : (j + 1) * block] = value.astype(bf16)
            if i != j:
                offset[j * block : (j + 1) * block, i * block : (i + 1) * block] = value.T.astype(bf16)

    mine = pl.ds(pl.multiple_of(me * width, 128), width)

    @pl.loop(0, states // block)
    def _(r):
        rows = span(r, block)
        value = dot32(offset[rows, :], offset[:, mine])
        second[rows, :] = value
        term[rows, :] = value.astype(bf16)

    @pl.loop(0, states // block)
    def _(r):
        rows = span(r, block)
        value = dot32(offset[rows, :], term[...])
        third[rows, :] = (value / 16.0 - second[rows, :] * (5.0 / 16.0)).astype(bf16)

    @pl.loop(0, states // block)
    def _(r):
        rows = span(r, block)
        tail = dot32(offset[rows, :], third[...])
        first = offset[rows, mine].astype(f32)
        change_ref[rows, :] = (tail + 0.375 * second[rows, :] - 0.5 * first).astype(bf16)

    for h in range(2):
        filtered_copy(h).wait()
    for i in range(4):
        everyone_copy(i).wait()


def rotate_kernel(filtered_ref, everyone_ref, change_ref, scale_ref, out_ref):
    block = everyone_ref.shape[2]
    value = jnp.concatenate([filtered_ref[0], filtered_ref[1]], axis=1)
    for q in range(4):
        value = value + dot32(everyone_ref[q], change_ref[q * block : (q + 1) * block, :])
    out_ref[...] = value * scale_ref[0:1, 0:1]


def fused(wavefunctions, mass_scale, cell_matrices, connectivity, face_index, domains):
    bf16, f32 = jnp.bfloat16, jnp.float32
    own, width = wavefunctions.shape
    face = face_index.shape[0]
    cells, nodes = connectivity.shape
    extent, share = own + face, (own + face) // 2
    states, block = 2 * width, width // 2
    inner, outer = split_domains(domains)
    slab = block // inner
    piece = slab // outer
    vmem = pl.BlockSpec(memory_space=pltpu.VMEM)
    hbm = pl.BlockSpec(memory_space=pl.ANY)
    dma = pltpu.SemaphoreType.DMA
    scratch = dict(
        matrix=pltpu.VMEM((extent, extent), bf16),
        b=pltpu.VMEM((cells * nodes, share), bf16),
        picks=pltpu.VMEM((share, nodes), bf16),
        hits=pltpu.VMEM((face, cells * nodes), bf16),
        mass_all=pltpu.VMEM((own, 128), f32),
        face_column=pltpu.VMEM((face, 128), jnp.int32),
        face_of=pltpu.VMEM((face, own), bf16),
        face_in=pltpu.VMEM((own, face), bf16),
        scaled=pltpu.VMEM((2, own, block), bf16),
        sent=pltpu.VMEM((3, 2, 2 * face, block), bf16),
        returned_in=pltpu.VMEM((3, 2, face, block), bf16),
        faces_in=pltpu.VMEM((3, 2, face, block), bf16),
        corner_in=pltpu.VMEM((face, face), bf16),
        rests=pltpu.VMEM((2, extent, 128), bf16),
        rest_all=pltpu.VMEM((own, 128), f32),
        corner_rest=pltpu.VMEM((face, 128), bf16),
        corner_rest_in=pltpu.VMEM((face, 128), bf16),
        added_low=pltpu.VMEM((face, block), bf16),
        states_one=pltpu.VMEM((2, own, block), f32),
        states_two=pltpu.VMEM((2, own, block), f32),
        everyone=pltpu.VMEM((4, own, block), bf16),
        part=pltpu.VMEM((5, block, block), bf16),
        first_in=pltpu.VMEM((5, inner - 1, slab, block), bf16),
        first_sum=pltpu.VMEM((5, slab, block), bf16),
        second_in=pltpu.VMEM((5, outer - 1, piece, block), bf16),
        gathered=pltpu.VMEM((2, 5, block, block), bf16),
        offset=pltpu.VMEM((states, states), bf16),
        second=pltpu.VMEM((states, width), f32),
        third=pltpu.VMEM((states, width), bf16),
        term=pltpu.VMEM((states, width), bf16),
        local_sem=dma((6,)),
    )
    counts = dict(
        face=(3, 2), corner=(2,), matrix=(extent // face,), rest=(extent // face,), band=(2,),
        one=(5, inner - 1), two=(5, outer - 1), three=(5, outer - 1), four=(5, inner - 1), five=(5,),
    )
    counts["return"] = (3, 2)
    for name, shape in counts.items():
        scratch[name + "_send"] = dma(shape)
        scratch[name + "_recv"] = dma(shape)
    names = ("conn", "a", "mass", "face", "wave", "everyone_out", "filtered_out", "change", "scale")
    everyone, filtered, change, scale = pl.pallas_call(
        functools.partial(fused_kernel, inner, outer, names + tuple(scratch)),
        out_shape=(
            jax.ShapeDtypeStruct((4, own, block), bf16),
            jax.ShapeDtypeStruct((2, own, block), f32),
            jax.ShapeDtypeStruct((states, width), bf16),
            jax.ShapeDtypeStruct((8, 128), f32),
        ),
        in_specs=[vmem] * 5,
        out_specs=(hbm, hbm, vmem, vmem),
        scratch_shapes=list(scratch.values()),
        compiler_params=pltpu.CompilerParams(
            vmem_limit_bytes=FUSED_LIMIT, collective_id=1, has_side_effects=True
        ),
        name="fused",
    )(connectivity, cell_matrices, mass_scale[None, :], face_index[None, :], wavefunctions)
    tile = face
    return pl.pallas_call(
        rotate_kernel,
        grid=(own // tile,),
        out_shape=jax.ShapeDtypeStruct((own, width), f32),
        in_specs=[
            pl.BlockSpec((2, tile, block), lambda i: (0, i, 0)),
            pl.BlockSpec((4, tile, block), lambda i: (0, i, 0)),
            pl.BlockSpec((states, width), lambda i: (0, 0)),
            pl.BlockSpec((8, 128), lambda i: (0, 0)),
        ],
        out_specs=pl.BlockSpec((tile, width), lambda i: (i, 0)),
        name="rotate",
    )(filtered, everyone, change, scale)


def fits(own, width, face, domains):
    return (
        lax.axis_size("band") == 2
        and min(split_domains(domains)) > 1
        and width % (32 * domains) == 0
        and width % 256 == 0
        and face % 128 == 0
        and own % face == 0
        and (own + face) % 256 == 0
    )


def passed_along(value, axis, steps):
    count = lax.axis_size(axis)
    initial, last = (max(0, -steps), min(count, count - steps))
    return lax.ppermute(value, axis, [(source, source + steps) for source in range(initial, last)])


def on_device(wavefunctions, mass_scale, cell_matrices, connectivity, face_index):
    bf16 = jnp.bfloat16
    own, band_width = wavefunctions.shape
    face = face_index.shape[0]
    domains = lax.axis_size("dom")
    states = band_width * lax.axis_size("band")
    if fits(own, band_width, face, domains):
        return fused(wavefunctions, mass_scale, cell_matrices, connectivity, face_index, domains)
    matrix, rest = domain_operator(cell_matrices, connectivity, own + face)
    face_of = (face_index[:, None] == lax.broadcasted_iota(jnp.int32, (face, own), 1)).astype(bf16)
    face_in = (face_index[None, :] == lax.broadcasted_iota(jnp.int32, (own, face), 0)).astype(bf16)
    outgoing = jnp.concatenate([matrix[own:, :own], face_of], axis=0)
    inner = matrix[:own, :own]
    edge = jnp.concatenate([matrix[:own, own:], face_in, face_in], axis=1)
    corner = jnp.concatenate([matrix[own:, own:], rest[own:].astype(bf16)], axis=1)
    corner = passed_along(corner, "dom", 1)
    corner, corner_rest = corner[:, :face], corner[:, face : face + 1].astype(jnp.float32)
    rest = rest[:own, :1]
    mass = mass_scale[:, None]

    def hamiltonian(vectors):
        scaled = (mass * vectors).astype(bf16)
        sent = dot32(outgoing, scaled).astype(bf16)
        returned = passed_along(sent[:face], "dom", 1)
        received = passed_along(sent[face:], "dom", -1)
        summed = dot32(inner, scaled) + rest * scaled.astype(jnp.float32)
        added = returned.astype(jnp.float32) + dot32(corner, sent[face:])
        added = added + corner_rest * sent[face:].astype(jnp.float32)
        high = added.astype(bf16)
        low = (added - lax.reduce_precision(added, 8, 7)).astype(bf16)
        summed = summed + dot32(edge, jnp.concatenate([received, high, low], axis=0))
        return mass * summed

    previous = wavefunctions.astype(jnp.float32)
    current = (hamiltonian(previous) - filter_center * previous) / filter_half
    for _ in range(2):
        following = 2.0 * (hamiltonian(current) - filter_center * current) / filter_half - previous
        previous, current = (current, following)
    rounded = current.astype(bf16)
    everyone = lax.all_gather(rounded, "band", axis=1, tiled=True)
    partial = dot32(everyone, rounded, ((0,), (0,))) / (own * domains)
    tile = lax.psum_scatter(partial.astype(bf16), "dom", scatter_dimension=0, tiled=True)
    columns = lax.all_gather(tile, "dom", axis=0, tiled=True)
    margin = lax.all_gather(columns, "band", axis=1, tiled=True).astype(jnp.float32)
    identity = (
        lax.broadcasted_iota(jnp.int32, (states, states), 0)
        == lax.broadcasted_iota(jnp.int32, (states, states), 1)
    ).astype(jnp.float32)
    mean_eigen = jnp.sum(margin * identity) / states
    offset = (margin / mean_eigen - identity).astype(bf16)
    start = lax.axis_index("band") * band_width
    first = lax.dynamic_slice_in_dim(columns.astype(jnp.float32), 0, states, 0) / mean_eigen
    first = first - lax.dynamic_slice_in_dim(identity, start, band_width, 1)
    second = dot32(offset, first.astype(bf16))
    third = dot32(offset, second.astype(bf16))
    tail = dot32(offset, (third / 16.0 - second * (5.0 / 16.0)).astype(bf16))
    change = tail + 0.375 * second - 0.5 * first
    turned = current + dot32(everyone, change.astype(bf16))
    return turned / jnp.sqrt(mean_eigen)


def solution(mesh):
    return jax.shard_map(
        on_device,
        mesh=mesh,
        in_specs=(P("dom", "band"), P("dom"), P("dom", None, None), P("dom", None), P("dom")),
        out_specs=P("dom", "band"),
        check_vma=False,
    )
```

```python
import functools

import jax
import jax.numpy as jnp
from jax import lax
from jax.experimental import pallas as pl
from jax.experimental.pallas import tpu as pltpu
from jax.sharding import PartitionSpec as P

filter_center = 5.0
filter_half = 5.0
MESH = pl.DeviceIdType.MESH
VMEM_LIMIT = 62 * 1024 * 1024
FUSED_LIMIT = 67043328


def row_tile(rows, most):
    return max(t for t in range(16, most + 1, 16) if rows % t == 0)


def dot32(a, b, dims=((1,), (0,))):
    return lax.dot_general(a, b, (dims, ((), ())), preferred_element_type=jnp.float32)


def operator_kernel(share, conn_ref, a_ref, m_ref, ht, b, send_sem, recv_sem):
    cells, nodes = conn_ref.shape
    extent, width = m_ref.shape[1], b.shape[1]
    me = lax.axis_index("band") if share > 1 else 0
    if share > 1:
        barrier = pltpu.get_barrier_semaphore()
        for step in range(1, share):
            peer = lax.rem(me + step, share)
            pl.semaphore_signal(barrier, inc=1, device_id={"band": peer}, device_id_type=MESH)
        pl.semaphore_wait(barrier, share - 1)
    build = row_tile(extent, 256)

    @pl.loop(0, cells)
    def _(c):
        links = conn_ref[pl.ds(c, 1), :]
        span = pl.ds(pl.multiple_of(c * nodes, 128), nodes)

        @pl.loop(0, extent // build)
        def _(r):
            ids = lax.broadcasted_iota(jnp.int32, (build, nodes), 0) + r * build
            ht[pl.ds(pl.multiple_of(r * build, build), build), span] = jnp.where(
                ids == links, 1.0, 0.0
            ).astype(jnp.bfloat16)

    first = pl.multiple_of(me * width, 128) if share > 1 else 0

    @pl.loop(0, cells)
    def _(c):
        span = pl.ds(pl.multiple_of(c * nodes, 128), nodes)
        picks = ht[pl.ds(first, width), span]
        b[span, :] = dot32(a_ref[c], picks, ((1,), (1,))).astype(jnp.bfloat16)

    tile = row_tile(extent, 384)
    tiles = extent // tile

    def copies(r):
        rows = pl.ds(pl.multiple_of(r * tile, tile), tile)
        return [
            pltpu.make_async_remote_copy(
                src_ref=m_ref.at[me, rows],
                dst_ref=m_ref.at[me, rows],
                send_sem=send_sem.at[step, r],
                recv_sem=recv_sem.at[step, r],
                device_id={"band": lax.rem(me + step, share)},
                device_id_type=MESH,
            )
            for step in range(1, share)
        ]

    @pl.loop(0, tiles)
    def _(r):
        rows = pl.ds(pl.multiple_of(r * tile, tile), tile)
        total = dot32(ht[rows, :], b[...])
        kept = total.astype(jnp.bfloat16)
        m_ref[me, rows, :width] = kept
        offsets = lax.broadcasted_iota(jnp.int32, (tile, width), 1) - lax.broadcasted_iota(
            jnp.int32, (tile, width), 0
        )
        rest = jnp.where(
            offsets == r * tile - me * width, total - kept.astype(jnp.float32), 0.0
        )
        rest = jnp.sum(rest, axis=1, keepdims=True)
        m_ref[me, rows, width:] = jnp.broadcast_to(rest, (tile, 128)).astype(jnp.bfloat16)
        for copy in copies(r):
            copy.start()

    @pl.loop(0, tiles)
    def _(r):
        for copy in copies(r):
            copy.wait()


def domain_operator(cell_matrices, connectivity, extent):
    cells, nodes = connectivity.shape
    share = lax.axis_size("band")
    if extent % (share * 128):
        share = 1
    width = extent // share
    tiles = extent // row_tile(extent, 384)
    vmem = pl.BlockSpec(memory_space=pltpu.VMEM)
    params = dict(collective_id=0, has_side_effects=True) if share > 1 else {}
    halves = pl.pallas_call(
        functools.partial(operator_kernel, share),
        out_shape=jax.ShapeDtypeStruct((share, extent, width + 128), jnp.bfloat16),
        in_specs=[vmem] * 2,
        out_specs=vmem,
        scratch_shapes=[
            pltpu.VMEM((extent, cells * nodes), jnp.bfloat16),
            pltpu.VMEM((cells * nodes, width), jnp.bfloat16),
            pltpu.SemaphoreType.DMA((share, tiles)),
            pltpu.SemaphoreType.DMA((share, tiles)),
        ],
        compiler_params=pltpu.CompilerParams(vmem_limit_bytes=VMEM_LIMIT, **params),
        name="domain_operator",
    )(connectivity, cell_matrices)
    rest = sum(halves[i, :, width:].astype(jnp.float32) for i in range(share))
    return jnp.concatenate([halves[i, :, :width] for i in range(share)], axis=1), rest


def upper_blocks(band):
    other = 1 - band
    return (
        (2 * band, 2 * band),
        (2 * band, 2 * band + 1),
        (2 * band + 1, 2 * band + 1),
        (2 * band, 2 * other + band),
        (2 * band + 1, 2 * other + 1 - band),
    )


def split_domains(domains):
    inner = max(n for n in range(1, domains + 1) if domains % n == 0 and n * n <= domains)
    return inner, domains // inner


def column_form(row):
    return jnp.broadcast_to(row, (128, 128)).T


def one_hot(ids, links):
    return jnp.where(ids == links, 1.0, 0.0).astype(jnp.bfloat16)


def span(index, size):
    return pl.ds(pl.multiple_of(index * size, size), size)


def fused_kernel(inner, outer, names, *args):
    refs = dict(zip(names, args))
    conn_ref, a_ref, mass_ref, face_ref, wave_ref = (refs[n] for n in names[:5])
    out_ref, change = refs[names[5]], refs["term"]
    matrix, b, picks, picks_next, hits = (
        refs[n] for n in ("matrix", "b", "picks", "picks_next", "hits")
    )
    mass_all, face_column, face_of, face_in = (
        refs[n] for n in ("mass_all", "face_column", "face_of", "face_in")
    )
    scaled, sent, returned_in, faces_in, corner_in = (
        refs[n] for n in ("scaled", "sent", "returned_in", "faces_in", "corner_in")
    )
    lost = refs["lost"]
    rests, rest_all, corner_rest, corner_rest_in, added_low = (
        refs[n] for n in ("rests", "rest_all", "corner_rest", "corner_rest_in", "added_low")
    )
    states_one, states_two, everyone = (refs[n] for n in ("states_one", "states_two", "everyone"))
    part, first_in, first_sum, second_in, gathered = (
        refs[n] for n in ("part", "first_in", "first_sum", "second_in", "gathered")
    )
    offset, second, third, term = (refs[n] for n in ("offset", "second", "third", "term"))
    bf16, f32 = jnp.bfloat16, jnp.float32
    cells, nodes = conn_ref.shape
    own, width = wave_ref.shape
    face = face_ref.shape[1]
    extent = own + face
    states, block = 2 * width, width // 2
    share = extent // 2
    domains = inner * outer
    slab, piece = block // inner, block // inner // outer
    chunks = 5
    me = lax.axis_index("band")
    dom = lax.axis_index("dom")
    high, low = dom // inner, lax.rem(dom, inner)
    partner = 1 - me
    after, before = lax.rem(dom + 1, domains), lax.rem(dom + domains - 1, domains)
    plane = [high * inner + lax.rem(low + step, inner) for step in range(1, inner)]
    line = [lax.rem(high + step, outer) * inner + low for step in range(1, outer)]
    has_after, has_before = dom < domains - 1, dom > 0

    barrier = pltpu.get_barrier_semaphore()
    for peer in plane + line + [after, before]:
        pl.semaphore_signal(barrier, inc=1, device_id={"dom": peer}, device_id_type=MESH)
    pl.semaphore_signal(barrier, inc=1, device_id={"band": partner}, device_id_type=MESH)

    def remote(source, target, name, *at, **where):
        return pltpu.make_async_remote_copy(
            src_ref=source, dst_ref=target,
            send_sem=refs[name + "_send"].at[at], recv_sem=refs[name + "_recv"].at[at],
            device_id=where, device_id_type=MESH,
        )

    @pl.loop(0, own // 128)
    def _(i):
        mass_all[span(i, 128), :] = column_form(mass_ref[:, span(i, 128)])

    for i in range(face // 128):
        face_column[i * 128 : (i + 1) * 128, :] = column_form(
            face_ref[:, i * 128 : (i + 1) * 128].astype(f32)
        ).astype(jnp.int32)

    @pl.loop(0, own // 128)
    def _(i):
        ids = lax.broadcasted_iota(jnp.int32, (face, 128), 1) + i * 128
        face_of[:, span(i, 128)] = one_hot(ids, face_column[...])
        ids = lax.broadcasted_iota(jnp.int32, (128, face), 0) + i * 128
        face_in[span(i, 128), :] = one_hot(ids, face_ref[...])

    def wide(value):
        return jnp.concatenate([value] * (block // 128), axis=1)

    def mass_tile(rows):
        return wide(mass_all[rows, :])

    @pl.loop(0, own // face)
    def _(t):
        rows = span(t, face)
        for h in range(2):
            value = wave_ref[rows, h * block : (h + 1) * block].astype(f32)
            scaled[h, rows, :] = (mass_tile(rows) * value).astype(bf16)

    for k in range(3):
        for h in range(2):
            @pl.when(jnp.logical_not(has_after))
            def _():
                faces_in[k, h] = jnp.zeros_like(faces_in[k, h])

            @pl.when(jnp.logical_not(has_before))
            def _():
                returned_in[k, h] = jnp.zeros_like(returned_in[k, h])

    @pl.when(jnp.logical_not(has_before))
    def _():
        corner_in[...] = jnp.zeros_like(corner_in)
        corner_rest_in[...] = jnp.zeros_like(corner_rest_in)

    def face_copy(k, h):
        return remote(sent.at[k, h, pl.ds(face, face)], faces_in.at[k, h], "face", k, h, dom=before)

    def return_copy(k, h):
        return remote(sent.at[k, h, pl.ds(0, face)], returned_in.at[k, h], "return", k, h, dom=after)

    def corner_copy():
        source = matrix.at[pl.ds(own, face), pl.ds(own, face)]
        return remote(source, corner_in, "corner", 0, dom=after)

    def corner_rest_copy():
        return remote(corner_rest, corner_rest_in, "corner", 1, dom=after)

    def send_faces(k, h):
        sent[k, h, face:] = dot32(face_of[...], scaled[h]).astype(bf16)

        @pl.when(has_before)
        def _():
            face_copy(k, h).start()

    def send_returned(k, h):
        sent[k, h, :face] = dot32(matrix[own:, :own], scaled[h]).astype(bf16)

        @pl.when(has_after)
        def _():
            return_copy(k, h).start()

    pl.semaphore_wait(barrier, inner + outer + 1)
    for h in range(2):
        send_faces(0, h)

    columns = pl.ds(pl.multiple_of(me * share, 128), share)

    def pick(target, c):
        links = conn_ref[pl.ds(c, 1), :].astype(f32)
        for i in range(nodes // 128):
            rows = slice(i * 128, (i + 1) * 128)
            numbers = column_form(links[:, rows]).astype(jnp.int32)
            for j in range(share // 128):
                ids = lax.broadcasted_iota(jnp.int32, (128, 128), 1) + (j * 128 + me * share)
                target[rows, j * 128 : (j + 1) * 128] = one_hot(ids, numbers)

    def cell(c, picked):
        half = nodes // 2
        for i in range(2):
            rows = slice(i * half, (i + 1) * half)
            value = dot32(a_ref[c, rows, :], picked[...])
            kept = value.astype(bf16)
            b[pl.ds(pl.multiple_of(c * nodes + i * half, half), half), :] = kept
            left = (value - kept.astype(f32)) * picked[rows, :].astype(f32)
            lost[...] += jnp.sum(left.reshape(half // 8, 8, share), axis=0)

    pick(picks, 0)
    lost[...] = jnp.zeros_like(lost)

    @pl.loop(0, cells // 2)
    def _(g):
        pick(picks_next, 2 * g + 1)
        cell(2 * g, picks)
        pick(picks, jnp.minimum(2 * g + 2, cells - 1))
        cell(2 * g + 1, picks_next)

    rest_all[...] = jnp.zeros_like(rest_all)
    for j in range(share // 128):
        row = jnp.sum(lost[:, j * 128 : (j + 1) * 128], axis=0, keepdims=True)
        rest_all[pl.ds(pl.multiple_of(me * share + j * 128, 128), 128), :] = column_form(row)

    tiles = extent // face

    def matrix_copy(r):
        spot = matrix.at[span(tiles - 1 - r, face), columns]
        return remote(spot, spot, "matrix", r, band=partner)

    def rest_copy(r):
        spot = rests.at[me, span(tiles - 1 - r, face)]
        return remote(spot, spot, "rest", r, band=partner)

    @pl.loop(0, tiles)
    def _(r):
        t = tiles - 1 - r
        for c in range(cells):
            ids = lax.broadcasted_iota(jnp.int32, (face, nodes), 0) + t * face
            hits[:, c * nodes : (c + 1) * nodes] = one_hot(ids, conn_ref[c : c + 1, :])
        total = dot32(hits[...], b[...])
        kept = total.astype(bf16)
        matrix[span(t, face), columns] = kept
        gaps = lax.broadcasted_iota(jnp.int32, (face, share), 1) - lax.broadcasted_iota(
            jnp.int32, (face, share), 0
        )
        rest = jnp.where(gaps == t * face - me * share, total - kept.astype(f32), 0.0)
        rest = jnp.sum(rest, axis=1, keepdims=True)
        rests[me, span(t, face), :] = (rest + rest_all[span(t, face), :]).astype(bf16)
        matrix_copy(r).start()
        rest_copy(r).start()

        @pl.when(r == 1)
        def _():
            matrix_copy(0).wait()
            rest_copy(0).wait()
            corner_rest[...] = rests[0, own:, :] + rests[1, own:, :]

            @pl.when(has_after)
            def _():
                corner_copy().start()
                corner_rest_copy().start()

            for h in range(2):
                send_returned(0, h)

    @pl.loop(1, tiles)
    def _(r):
        matrix_copy(r).wait()
        rest_copy(r).wait()

    @pl.loop(0, own // face)
    def _(t):
        rows = span(t, face)
        rest_all[rows, :] = rests[0, rows, :].astype(f32) + rests[1, rows, :].astype(f32)

    tall = own // max(1, own // (2 * face))
    ratio = 1.0 / filter_half
    shift = filter_center / filter_half

    def wave_tile(h, rows):
        return wave_ref[rows, h * block : (h + 1) * block].astype(f32)

    def advance(k, h):
        target = states_two if k == 1 else states_one

        @pl.loop(0, own // tall)
        def _(t):
            rows = span(t, tall)
            value = dot32(matrix[rows, :own], scaled[h])
            value = value + wide(rest_all[rows, :]) * scaled[h, rows, :].astype(f32)
            value = value * mass_tile(rows)
            if k == 0:
                target[h, rows, :] = ratio * value - shift * wave_tile(h, rows)
            elif k == 1:
                target[h, rows, :] = (
                    2.0 * ratio * value - 2.0 * shift * states_one[h, rows, :] - wave_tile(h, rows)
                )
            else:
                target[h, rows, :] = (
                    2.0 * ratio * value - 2.0 * shift * states_two[h, rows, :] - states_one[h, rows, :]
                )

        def wait_both(copies):
            for copy, sends, receives in copies:
                @pl.when(sends)
                def _():
                    copy.wait_send()

                @pl.when(receives)
                def _():
                    copy.wait_recv()

        waits = [(face_copy(k, h), has_before, has_after), (return_copy(k, h), has_after, has_before)]
        if k == 0 and h == 0:
            waits.append((corner_copy(), has_after, has_before))
            waits.append((corner_rest_copy(), has_after, has_before))
        wait_both(waits)
        added = returned_in[k, h].astype(f32) + dot32(corner_in[...], sent[k, h, face:])
        added = added + wide(corner_rest_in[...].astype(f32)) * sent[k, h, face:].astype(f32)
        kept = added.astype(bf16)
        sent[k, h, :face] = kept
        added_low[...] = (added - kept.astype(f32)).astype(bf16)
        scale = ratio if k == 0 else 2.0 * ratio

        @pl.loop(0, own // tall)
        def _(t):
            rows = span(t, tall)
            value = dot32(matrix[rows, own:], faces_in[k, h]) + dot32(face_in[rows, :], sent[k, h, :face])
            value = value + dot32(face_in[rows, :], added_low[...])
            mass = mass_tile(rows)
            value = target[h, rows, :] + scale * value * mass
            target[h, rows, :] = value
            if k < 2:
                scaled[h, rows, :] = (mass * value).astype(bf16)
            else:
                everyone[2 * me + h, rows, :] = value.astype(bf16)

    def band_copy(h):
        spot = everyone.at[2 * me + h]
        return remote(spot, spot, "band", h, band=partner)

    def local(source, target, index):
        return pltpu.make_async_copy(source, target, refs["local_sem"].at[index])

    def out_copy(t, h):
        target = out_ref.at[span(t, face), pl.ds(h * block, block)]
        return local(states_two.at[h, span(t, face)], target, 2 * t + h)

    def plane_copies(c):
        return [
            remote(
                part.at[c, span(lax.rem(low + step, inner), slab)],
                first_in.at[c, step - 1], "one", c, step - 1, dom=plane[step - 1],
            )
            for step in range(1, inner)
        ]

    def line_copies(c):
        return [
            remote(
                first_sum.at[c, span(lax.rem(high + step, outer), piece)],
                second_in.at[c, step - 1], "two", c, step - 1, dom=line[step - 1],
            )
            for step in range(1, outer)
        ]

    own_slab = span(low, slab)
    own_piece = pl.ds(pl.multiple_of(low * slab + high * piece, piece), piece)

    def line_back(c):
        spot = gathered.at[me, c, own_piece]
        return [remote(spot, spot, "three", c, s - 1, dom=line[s - 1]) for s in range(1, outer)]

    def plane_back(c):
        spot = gathered.at[me, c, own_slab]
        return [remote(spot, spot, "four", c, s - 1, dom=plane[s - 1]) for s in range(1, inner)]

    def band_back(c):
        spot = gathered.at[me, c]
        return remote(spot, spot, "five", c, band=partner)

    def emit(c, left, right):
        value = dot32(everyone[left], everyone[right], ((0,), (0,)))
        part[c] = (value * (1.0 / (own * domains))).astype(bf16)
        for copy in plane_copies(c):
            copy.start()

    for k in range(3):
        for h in range(2):
            advance(k, h)
            if k < 2:
                send_faces(k + 1, h)
                send_returned(k + 1, h)
            else:
                band_copy(h).start()
                if h == 0:
                    emit(0, 2 * me, 2 * me)
    emit(1, 2 * me, 2 * me + 1)
    emit(2, 2 * me + 1, 2 * me + 1)
    for h in range(2):
        band_copy(h).wait()
    for i in range(2):
        emit(3 + i, 2 * me + i, 2 * partner + i + me - 2 * i * me)

    for c in range(chunks):
        total = part[c, own_slab].astype(f32)
        for step, copy in enumerate(plane_copies(c)):
            copy.wait()
            total = total + first_in[c, step].astype(f32)
        first_sum[c] = total.astype(bf16)
        for copy in line_copies(c):
            copy.start()
    for c in range(chunks):
        total = first_sum[c, span(high, piece)].astype(f32)
        for step, copy in enumerate(line_copies(c)):
            copy.wait()
            total = total + second_in[c, step].astype(f32)
        gathered[me, c, own_piece] = total.astype(bf16)
        for copy in line_back(c):
            copy.start()
    for c in range(chunks):
        for copy in line_back(c):
            copy.wait()
        for copy in plane_back(c):
            copy.start()
    for c in range(chunks):
        for copy in plane_back(c):
            copy.wait()
        band_back(c).start()
    for c in range(chunks):
        band_back(c).wait()

    unit = (
        lax.broadcasted_iota(jnp.int32, (block, block), 0)
        == lax.broadcasted_iota(jnp.int32, (block, block), 1)
    ).astype(f32)
    trace = 0.0
    for q in range(2):
        for c in (0, 2):
            trace = trace + jnp.sum(gathered[q, c].astype(f32) * unit)
    mean_eigen = jnp.full((1, 1), trace, f32) / states
    inverse = 1.0 / mean_eigen
    scale = lax.rsqrt(mean_eigen)
    for q in range(2):
        for c, (i, j) in enumerate(upper_blocks(q)):
            value = gathered[q, c].astype(f32) * inverse
            if i == j:
                value = value - unit
            offset[i * block : (i + 1) * block, j * block : (j + 1) * block] = value.astype(bf16)
            if i != j:
                offset[j * block : (j + 1) * block, i * block : (i + 1) * block] = value.T.astype(bf16)

    mine = pl.ds(pl.multiple_of(me * width, 128), width)

    @pl.loop(0, states // block)
    def _(r):
        rows = span(r, block)
        value = dot32(offset[rows, :], offset[:, mine])
        second[rows, :] = value
        term[rows, :] = value.astype(bf16)

    @pl.loop(0, states // block)
    def _(r):
        rows = span(r, block)
        value = dot32(offset[rows, :], term[...])
        third[rows, :] = (value / 16.0 - second[rows, :] * (5.0 / 16.0)).astype(bf16)

    @pl.loop(0, states // block)
    def _(r):
        rows = span(r, block)
        tail = dot32(offset[rows, :], third[...])
        first = offset[rows, mine].astype(f32)
        change[rows, :] = (tail + 0.375 * second[rows, :] - 0.5 * first).astype(bf16)

    @pl.loop(0, own // face)
    def _(t):
        rows = span(t, face)
        value = jnp.concatenate([states_one[0, rows, :], states_one[1, rows, :]], axis=1)
        for q in range(4):
            value = value + dot32(everyone[q, rows, :], change[q * block : (q + 1) * block, :])
        value = value * scale
        for h in range(2):
            states_two[h, rows, :] = value[:, h * block : (h + 1) * block]
            out_copy(t, h).start()

    @pl.loop(0, own // face)
    def _(t):
        for h in range(2):
            out_copy(t, h).wait()


def fused(wavefunctions, mass_scale, cell_matrices, connectivity, face_index, domains):
    bf16, f32 = jnp.bfloat16, jnp.float32
    own, width = wavefunctions.shape
    face = face_index.shape[0]
    cells, nodes = connectivity.shape
    extent, share = own + face, (own + face) // 2
    states, block = 2 * width, width // 2
    inner, outer = split_domains(domains)
    slab = block // inner
    piece = slab // outer
    vmem = pl.BlockSpec(memory_space=pltpu.VMEM)
    hbm = pl.BlockSpec(memory_space=pl.ANY)
    dma = pltpu.SemaphoreType.DMA
    scratch = dict(
        matrix=pltpu.VMEM((extent, extent), bf16),
        b=pltpu.VMEM((cells * nodes, share), bf16),
        picks=pltpu.VMEM((nodes, share), bf16),
        picks_next=pltpu.VMEM((nodes, share), bf16),
        hits=pltpu.VMEM((face, cells * nodes), bf16),
        mass_all=pltpu.VMEM((own, 128), f32),
        face_column=pltpu.VMEM((face, 128), jnp.int32),
        face_of=pltpu.VMEM((face, own), bf16),
        face_in=pltpu.VMEM((own, face), bf16),
        scaled=pltpu.VMEM((2, own, block), bf16),
        sent=pltpu.VMEM((3, 2, 2 * face, block), bf16),
        returned_in=pltpu.VMEM((3, 2, face, block), bf16),
        faces_in=pltpu.VMEM((3, 2, face, block), bf16),
        corner_in=pltpu.VMEM((face, face), bf16),
        rests=pltpu.VMEM((2, extent, 128), bf16),
        rest_all=pltpu.VMEM((extent, 128), f32),
        lost=pltpu.VMEM((8, share), f32),
        corner_rest=pltpu.VMEM((face, 128), bf16),
        corner_rest_in=pltpu.VMEM((face, 128), bf16),
        added_low=pltpu.VMEM((face, block), bf16),
        states_one=pltpu.VMEM((2, own, block), f32),
        states_two=pltpu.VMEM((2, own, block), f32),
        everyone=pltpu.VMEM((4, own, block), bf16),
        part=pltpu.VMEM((5, block, block), bf16),
        first_in=pltpu.VMEM((5, inner - 1, slab, block), bf16),
        first_sum=pltpu.VMEM((5, slab, block), bf16),
        second_in=pltpu.VMEM((5, outer - 1, piece, block), bf16),
        gathered=pltpu.VMEM((2, 5, block, block), bf16),
        offset=pltpu.VMEM((states, states), bf16),
        second=pltpu.VMEM((states, width), f32),
        third=pltpu.VMEM((states, width), bf16),
        term=pltpu.VMEM((states, width), bf16),
        local_sem=dma((2 * own // face,)),
    )
    counts = dict(
        face=(3, 2), corner=(2,), matrix=(extent // face,), rest=(extent // face,), band=(2,),
        one=(5, inner - 1), two=(5, outer - 1), three=(5, outer - 1), four=(5, inner - 1), five=(5,),
    )
    counts["return"] = (3, 2)
    for name, shape in counts.items():
        scratch[name + "_send"] = dma(shape)
        scratch[name + "_recv"] = dma(shape)
    names = ("conn_ref", "a_ref", "mass_ref", "face_ref", "wave_ref", "out_ref")
    return pl.pallas_call(
        functools.partial(fused_kernel, inner, outer, names + tuple(scratch)),
        out_shape=jax.ShapeDtypeStruct((own, width), f32),
        in_specs=[vmem] * 5,
        out_specs=hbm,
        scratch_shapes=list(scratch.values()),
        compiler_params=pltpu.CompilerParams(
            vmem_limit_bytes=FUSED_LIMIT, collective_id=1, has_side_effects=True
        ),
        name="fused",
    )(connectivity, cell_matrices, mass_scale[None, :], face_index[None, :], wavefunctions)


def fits(own, width, face, cells, domains):
    return (
        lax.axis_size("band") == 2
        and min(split_domains(domains)) > 1
        and width % (32 * domains) == 0
        and width % 256 == 0
        and face % 128 == 0
        and own % face == 0
        and (own + face) % 256 == 0
        and cells % 2 == 0
    )


def passed_along(value, axis, steps):
    count = lax.axis_size(axis)
    initial, last = (max(0, -steps), min(count, count - steps))
    return lax.ppermute(value, axis, [(source, source + steps) for source in range(initial, last)])


def on_device(wavefunctions, mass_scale, cell_matrices, connectivity, face_index):
    bf16 = jnp.bfloat16
    own, band_width = wavefunctions.shape
    face = face_index.shape[0]
    domains = lax.axis_size("dom")
    states = band_width * lax.axis_size("band")
    if fits(own, band_width, face, connectivity.shape[0], domains):
        return fused(wavefunctions, mass_scale, cell_matrices, connectivity, face_index, domains)
    matrix, rest = domain_operator(cell_matrices, connectivity, own + face)
    face_of = (face_index[:, None] == lax.broadcasted_iota(jnp.int32, (face, own), 1)).astype(bf16)
    face_in = (face_index[None, :] == lax.broadcasted_iota(jnp.int32, (own, face), 0)).astype(bf16)
    outgoing = jnp.concatenate([matrix[own:, :own], face_of], axis=0)
    inner = matrix[:own, :own]
    edge = jnp.concatenate([matrix[:own, own:], face_in, face_in], axis=1)
    corner = jnp.concatenate([matrix[own:, own:], rest[own:].astype(bf16)], axis=1)
    corner = passed_along(corner, "dom", 1)
    corner, corner_rest = corner[:, :face], corner[:, face : face + 1].astype(jnp.float32)
    rest = rest[:own, :1]
    mass = mass_scale[:, None]

    def hamiltonian(vectors):
        scaled = (mass * vectors).astype(bf16)
        sent = dot32(outgoing, scaled).astype(bf16)
        returned = passed_along(sent[:face], "dom", 1)
        received = passed_along(sent[face:], "dom", -1)
        summed = dot32(inner, scaled) + rest * scaled.astype(jnp.float32)
        added = returned.astype(jnp.float32) + dot32(corner, sent[face:])
        added = added + corner_rest * sent[face:].astype(jnp.float32)
        high = added.astype(bf16)
        low = (added - lax.reduce_precision(added, 8, 7)).astype(bf16)
        summed = summed + dot32(edge, jnp.concatenate([received, high, low], axis=0))
        return mass * summed

    previous = wavefunctions.astype(jnp.float32)
    current = (hamiltonian(previous) - filter_center * previous) / filter_half
    for _ in range(2):
        following = 2.0 * (hamiltonian(current) - filter_center * current) / filter_half - previous
        previous, current = (current, following)
    rounded = current.astype(bf16)
    everyone = lax.all_gather(rounded, "band", axis=1, tiled=True)
    partial = dot32(everyone, rounded, ((0,), (0,))) / (own * domains)
    tile = lax.psum_scatter(partial.astype(bf16), "dom", scatter_dimension=0, tiled=True)
    columns = lax.all_gather(tile, "dom", axis=0, tiled=True)
    margin = lax.all_gather(columns, "band", axis=1, tiled=True).astype(jnp.float32)
    identity = (
        lax.broadcasted_iota(jnp.int32, (states, states), 0)
        == lax.broadcasted_iota(jnp.int32, (states, states), 1)
    ).astype(jnp.float32)
    mean_eigen = jnp.sum(margin * identity) / states
    offset = (margin / mean_eigen - identity).astype(bf16)
    start = lax.axis_index("band") * band_width
    first = lax.dynamic_slice_in_dim(columns.astype(jnp.float32), 0, states, 0) / mean_eigen
    first = first - lax.dynamic_slice_in_dim(identity, start, band_width, 1)
    second = dot32(offset, first.astype(bf16))
    third = dot32(offset, second.astype(bf16))
    tail = dot32(offset, (third / 16.0 - second * (5.0 / 16.0)).astype(bf16))
    change = tail + 0.375 * second - 0.5 * first
    turned = current + dot32(everyone, change.astype(bf16))
    return turned / jnp.sqrt(mean_eigen)


def solution(mesh):
    return jax.shard_map(
        on_device,
        mesh=mesh,
        in_specs=(P("dom", "band"), P("dom"), P("dom", None, None), P("dom", None), P("dom")),
        out_specs=P("dom", "band"),
        check_vma=False,
    )
```

```python
import functools

import jax
import jax.numpy as jnp
from jax import lax
from jax.experimental import pallas as pl
from jax.experimental.pallas import tpu as pltpu
from jax.sharding import PartitionSpec as P

filter_center = 5.0
filter_half = 5.0
MESH = pl.DeviceIdType.MESH
VMEM_LIMIT = 62 * 1024 * 1024
FUSED_LIMIT = 67043328


def row_tile(rows, most):
    return max(t for t in range(16, most + 1, 16) if rows % t == 0)


def dot32(a, b, dims=((1,), (0,))):
    return lax.dot_general(a, b, (dims, ((), ())), preferred_element_type=jnp.float32)


def operator_kernel(share, conn_ref, a_ref, m_ref, ht, b, send_sem, recv_sem):
    cells, nodes = conn_ref.shape
    extent, width = m_ref.shape[1], b.shape[1]
    me = lax.axis_index("band") if share > 1 else 0
    if share > 1:
        barrier = pltpu.get_barrier_semaphore()
        for step in range(1, share):
            peer = lax.rem(me + step, share)
            pl.semaphore_signal(barrier, inc=1, device_id={"band": peer}, device_id_type=MESH)
        pl.semaphore_wait(barrier, share - 1)
    build = row_tile(extent, 256)

    @pl.loop(0, cells)
    def _(c):
        links = conn_ref[pl.ds(c, 1), :]
        span = pl.ds(pl.multiple_of(c * nodes, 128), nodes)

        @pl.loop(0, extent // build)
        def _(r):
            ids = lax.broadcasted_iota(jnp.int32, (build, nodes), 0) + r * build
            ht[pl.ds(pl.multiple_of(r * build, build), build), span] = jnp.where(
                ids == links, 1.0, 0.0
            ).astype(jnp.bfloat16)

    first = pl.multiple_of(me * width, 128) if share > 1 else 0

    @pl.loop(0, cells)
    def _(c):
        span = pl.ds(pl.multiple_of(c * nodes, 128), nodes)
        picks = ht[pl.ds(first, width), span]
        b[span, :] = dot32(a_ref[c], picks, ((1,), (1,))).astype(jnp.bfloat16)

    tile = row_tile(extent, 384)
    tiles = extent // tile

    def copies(r):
        rows = pl.ds(pl.multiple_of(r * tile, tile), tile)
        return [
            pltpu.make_async_remote_copy(
                src_ref=m_ref.at[me, rows],
                dst_ref=m_ref.at[me, rows],
                send_sem=send_sem.at[step, r],
                recv_sem=recv_sem.at[step, r],
                device_id={"band": lax.rem(me + step, share)},
                device_id_type=MESH,
            )
            for step in range(1, share)
        ]

    @pl.loop(0, tiles)
    def _(r):
        rows = pl.ds(pl.multiple_of(r * tile, tile), tile)
        total = dot32(ht[rows, :], b[...])
        kept = total.astype(jnp.bfloat16)
        m_ref[me, rows, :width] = kept
        offsets = lax.broadcasted_iota(jnp.int32, (tile, width), 1) - lax.broadcasted_iota(
            jnp.int32, (tile, width), 0
        )
        rest = jnp.where(
            offsets == r * tile - me * width, total - kept.astype(jnp.float32), 0.0
        )
        rest = jnp.sum(rest, axis=1, keepdims=True)
        m_ref[me, rows, width:] = jnp.broadcast_to(rest, (tile, 128)).astype(jnp.bfloat16)
        for copy in copies(r):
            copy.start()

    @pl.loop(0, tiles)
    def _(r):
        for copy in copies(r):
            copy.wait()


def domain_operator(cell_matrices, connectivity, extent):
    cells, nodes = connectivity.shape
    share = lax.axis_size("band")
    if extent % (share * 128):
        share = 1
    width = extent // share
    tiles = extent // row_tile(extent, 384)
    vmem = pl.BlockSpec(memory_space=pltpu.VMEM)
    params = dict(collective_id=0, has_side_effects=True) if share > 1 else {}
    halves = pl.pallas_call(
        functools.partial(operator_kernel, share),
        out_shape=jax.ShapeDtypeStruct((share, extent, width + 128), jnp.bfloat16),
        in_specs=[vmem] * 2,
        out_specs=vmem,
        scratch_shapes=[
            pltpu.VMEM((extent, cells * nodes), jnp.bfloat16),
            pltpu.VMEM((cells * nodes, width), jnp.bfloat16),
            pltpu.SemaphoreType.DMA((share, tiles)),
            pltpu.SemaphoreType.DMA((share, tiles)),
        ],
        compiler_params=pltpu.CompilerParams(vmem_limit_bytes=VMEM_LIMIT, **params),
        name="domain_operator",
    )(connectivity, cell_matrices)
    rest = sum(halves[i, :, width:].astype(jnp.float32) for i in range(share))
    return jnp.concatenate([halves[i, :, :width] for i in range(share)], axis=1), rest


def upper_blocks(band):
    other = 1 - band
    return (
        (2 * band, 2 * band),
        (2 * band, 2 * band + 1),
        (2 * band + 1, 2 * band + 1),
        (2 * band, 2 * other + band),
        (2 * band + 1, 2 * other + 1 - band),
    )


def split_domains(domains):
    inner = max(n for n in range(1, domains + 1) if domains % n == 0 and n * n <= domains)
    return inner, domains // inner


def column_form(row):
    return jnp.broadcast_to(row, (128, 128)).T


def one_hot(ids, links):
    return jnp.where(ids == links, 1.0, 0.0).astype(jnp.bfloat16)


def span(index, size):
    return pl.ds(pl.multiple_of(index * size, size), size)


def fused_kernel(inner, outer, names, *args):
    refs = dict(zip(names, args))
    conn_ref, a_ref, mass_ref, face_ref, wave_ref = (refs[n] for n in names[:5])
    out_ref, scale_ref, change = refs[names[5]], refs[names[6]], refs["term"]
    matrix, b, picks, picks_next, hits = (
        refs[n] for n in ("matrix", "b", "picks", "picks_next", "hits")
    )
    mass_all, face_column, face_of, face_in = (
        refs[n] for n in ("mass_all", "face_column", "face_of", "face_in")
    )
    scaled, sent, returned_in, faces_in, corner_in = (
        refs[n] for n in ("scaled", "sent", "returned_in", "faces_in", "corner_in")
    )
    lost = refs["lost"]
    rests, rest_all, corner_rest, corner_rest_in, added_low = (
        refs[n] for n in ("rests", "rest_all", "corner_rest", "corner_rest_in", "added_low")
    )
    states_one, states_two, everyone = (refs[n] for n in ("states_one", "states_two", "everyone"))
    part, first_in, first_sum, second_in, gathered = (
        refs[n] for n in ("part", "first_in", "first_sum", "second_in", "gathered")
    )
    offset, second, third, term = (refs[n] for n in ("offset", "second", "third", "term"))
    bf16, f32 = jnp.bfloat16, jnp.float32
    cells, nodes = conn_ref.shape
    own, width = wave_ref.shape
    face = face_ref.shape[1]
    extent = own + face
    states, block = 2 * width, width // 2
    share = extent // 2
    domains = inner * outer
    slab, piece = block // inner, block // inner // outer
    chunks = 5
    me = lax.axis_index("band")
    dom = lax.axis_index("dom")
    high, low = dom // inner, lax.rem(dom, inner)
    partner = 1 - me
    after, before = lax.rem(dom + 1, domains), lax.rem(dom + domains - 1, domains)
    plane = [high * inner + lax.rem(low + step, inner) for step in range(1, inner)]
    line = [lax.rem(high + step, outer) * inner + low for step in range(1, outer)]
    has_after, has_before = dom < domains - 1, dom > 0

    barrier = pltpu.get_barrier_semaphore()
    for peer in plane + line + [after, before]:
        pl.semaphore_signal(barrier, inc=1, device_id={"dom": peer}, device_id_type=MESH)
    pl.semaphore_signal(barrier, inc=1, device_id={"band": partner}, device_id_type=MESH)

    def remote(source, target, name, *at, **where):
        return pltpu.make_async_remote_copy(
            src_ref=source, dst_ref=target,
            send_sem=refs[name + "_send"].at[at], recv_sem=refs[name + "_recv"].at[at],
            device_id=where, device_id_type=MESH,
        )

    @pl.loop(0, own // 128)
    def _(i):
        mass_all[span(i, 128), :] = column_form(mass_ref[:, span(i, 128)])

    for i in range(face // 128):
        face_column[i * 128 : (i + 1) * 128, :] = column_form(
            face_ref[:, i * 128 : (i + 1) * 128].astype(f32)
        ).astype(jnp.int32)

    @pl.loop(0, own // 128)
    def _(i):
        ids = lax.broadcasted_iota(jnp.int32, (face, 128), 1) + i * 128
        face_of[:, span(i, 128)] = one_hot(ids, face_column[...])
        ids = lax.broadcasted_iota(jnp.int32, (128, face), 0) + i * 128
        face_in[span(i, 128), :] = one_hot(ids, face_ref[...])

    def wide(value):
        return jnp.concatenate([value] * (block // 128), axis=1)

    def mass_tile(rows):
        return wide(mass_all[rows, :])

    @pl.loop(0, own // face)
    def _(t):
        rows = span(t, face)
        for h in range(2):
            value = wave_ref[rows, h * block : (h + 1) * block].astype(f32)
            scaled[h, rows, :] = (mass_tile(rows) * value).astype(bf16)

    for k in range(3):
        for h in range(2):
            @pl.when(jnp.logical_not(has_after))
            def _():
                faces_in[k, h] = jnp.zeros_like(faces_in[k, h])

            @pl.when(jnp.logical_not(has_before))
            def _():
                returned_in[k, h] = jnp.zeros_like(returned_in[k, h])

    @pl.when(jnp.logical_not(has_before))
    def _():
        corner_in[...] = jnp.zeros_like(corner_in)
        corner_rest_in[...] = jnp.zeros_like(corner_rest_in)

    def face_copy(k, h):
        return remote(sent.at[k, h, pl.ds(face, face)], faces_in.at[k, h], "face", k, h, dom=before)

    def return_copy(k, h):
        return remote(sent.at[k, h, pl.ds(0, face)], returned_in.at[k, h], "return", k, h, dom=after)

    def corner_copy():
        source = matrix.at[pl.ds(own, face), pl.ds(own, face)]
        return remote(source, corner_in, "corner", 0, dom=after)

    def corner_rest_copy():
        return remote(corner_rest, corner_rest_in, "corner", 1, dom=after)

    def send_faces(k, h):
        sent[k, h, face:] = dot32(face_of[...], scaled[h]).astype(bf16)

        @pl.when(has_before)
        def _():
            face_copy(k, h).start()

    def send_returned(k, h):
        sent[k, h, :face] = dot32(matrix[own:, :own], scaled[h]).astype(bf16)

        @pl.when(has_after)
        def _():
            return_copy(k, h).start()

    pl.semaphore_wait(barrier, inner + outer + 1)
    for h in range(2):
        send_faces(0, h)

    columns = pl.ds(pl.multiple_of(me * share, 128), share)

    def pick(target, c):
        links = conn_ref[pl.ds(c, 1), :].astype(f32)
        for i in range(nodes // 128):
            rows = slice(i * 128, (i + 1) * 128)
            numbers = column_form(links[:, rows]).astype(jnp.int32)
            for j in range(share // 128):
                ids = lax.broadcasted_iota(jnp.int32, (128, 128), 1) + (j * 128 + me * share)
                target[rows, j * 128 : (j + 1) * 128] = one_hot(ids, numbers)

    def cell(c, picked):
        half = nodes // 2
        for i in range(2):
            rows = slice(i * half, (i + 1) * half)
            value = dot32(a_ref[c, rows, :], picked[...])
            kept = value.astype(bf16)
            b[pl.ds(pl.multiple_of(c * nodes + i * half, half), half), :] = kept
            left = (value - kept.astype(f32)) * picked[rows, :].astype(f32)
            lost[...] += jnp.sum(left.reshape(half // 8, 8, share), axis=0)

    pick(picks, 0)
    lost[...] = jnp.zeros_like(lost)

    @pl.loop(0, cells // 2)
    def _(g):
        pick(picks_next, 2 * g + 1)
        cell(2 * g, picks)
        pick(picks, jnp.minimum(2 * g + 2, cells - 1))
        cell(2 * g + 1, picks_next)

    rest_all[...] = jnp.zeros_like(rest_all)
    for j in range(share // 128):
        row = jnp.sum(lost[:, j * 128 : (j + 1) * 128], axis=0, keepdims=True)
        rest_all[pl.ds(pl.multiple_of(me * share + j * 128, 128), 128), :] = column_form(row)

    tiles = extent // face

    def matrix_copy(r):
        spot = matrix.at[span(tiles - 1 - r, face), columns]
        return remote(spot, spot, "matrix", r, band=partner)

    def rest_copy(r):
        spot = rests.at[me, span(tiles - 1 - r, face)]
        return remote(spot, spot, "rest", r, band=partner)

    @pl.loop(0, tiles)
    def _(r):
        t = tiles - 1 - r
        for c in range(cells):
            ids = lax.broadcasted_iota(jnp.int32, (face, nodes), 0) + t * face
            hits[:, c * nodes : (c + 1) * nodes] = one_hot(ids, conn_ref[c : c + 1, :])
        total = dot32(hits[...], b[...])
        kept = total.astype(bf16)
        matrix[span(t, face), columns] = kept
        gaps = lax.broadcasted_iota(jnp.int32, (face, share), 1) - lax.broadcasted_iota(
            jnp.int32, (face, share), 0
        )
        rest = jnp.where(gaps == t * face - me * share, total - kept.astype(f32), 0.0)
        rest = jnp.sum(rest, axis=1, keepdims=True)
        rests[me, span(t, face), :] = (rest + rest_all[span(t, face), :]).astype(bf16)
        matrix_copy(r).start()
        rest_copy(r).start()

        @pl.when(r == 1)
        def _():
            matrix_copy(0).wait()
            rest_copy(0).wait()
            corner_rest[...] = rests[0, own:, :] + rests[1, own:, :]

            @pl.when(has_after)
            def _():
                corner_copy().start()
                corner_rest_copy().start()

            for h in range(2):
                send_returned(0, h)

    @pl.loop(1, tiles)
    def _(r):
        matrix_copy(r).wait()
        rest_copy(r).wait()

    @pl.loop(0, own // face)
    def _(t):
        rows = span(t, face)
        rest_all[rows, :] = rests[0, rows, :].astype(f32) + rests[1, rows, :].astype(f32)

    tall = own // max(1, own // (2 * face))
    ratio = 1.0 / filter_half
    shift = filter_center / filter_half

    def wave_tile(h, rows):
        return wave_ref[rows, h * block : (h + 1) * block].astype(f32)

    def advance(k, h):
        target = states_two if k == 1 else states_one

        @pl.loop(0, own // tall)
        def _(t):
            rows = span(t, tall)
            value = dot32(matrix[rows, :own], scaled[h])
            value = value + wide(rest_all[rows, :]) * scaled[h, rows, :].astype(f32)
            value = value * mass_tile(rows)
            if k == 0:
                target[h, rows, :] = ratio * value - shift * wave_tile(h, rows)
            elif k == 1:
                target[h, rows, :] = (
                    2.0 * ratio * value - 2.0 * shift * states_one[h, rows, :] - wave_tile(h, rows)
                )
            else:
                target[h, rows, :] = (
                    2.0 * ratio * value - 2.0 * shift * states_two[h, rows, :] - states_one[h, rows, :]
                )

        def wait_both(copies):
            for copy, sends, receives in copies:
                @pl.when(sends)
                def _():
                    copy.wait_send()

                @pl.when(receives)
                def _():
                    copy.wait_recv()

        waits = [(face_copy(k, h), has_before, has_after), (return_copy(k, h), has_after, has_before)]
        if k == 0 and h == 0:
            waits.append((corner_copy(), has_after, has_before))
            waits.append((corner_rest_copy(), has_after, has_before))
        wait_both(waits)
        added = returned_in[k, h].astype(f32) + dot32(corner_in[...], sent[k, h, face:])
        added = added + wide(corner_rest_in[...].astype(f32)) * sent[k, h, face:].astype(f32)
        kept = added.astype(bf16)
        sent[k, h, :face] = kept
        added_low[...] = (added - kept.astype(f32)).astype(bf16)
        scale = ratio if k == 0 else 2.0 * ratio

        @pl.loop(0, own // tall)
        def _(t):
            rows = span(t, tall)
            value = dot32(matrix[rows, own:], faces_in[k, h]) + dot32(face_in[rows, :], sent[k, h, :face])
            value = value + dot32(face_in[rows, :], added_low[...])
            mass = mass_tile(rows)
            value = target[h, rows, :] + scale * value * mass
            target[h, rows, :] = value
            if k < 2:
                scaled[h, rows, :] = (mass * value).astype(bf16)
            else:
                everyone[2 * me + h, rows, :] = value.astype(bf16)

    def band_copy(h):
        spot = everyone.at[2 * me + h]
        return remote(spot, spot, "band", h, band=partner)

    def local(source, target, index):
        return pltpu.make_async_copy(source, target, refs["local_sem"].at[index])

    def out_copy(t, h):
        target = out_ref.at[span(t, face), pl.ds(h * block, block)]
        return local(states_two.at[h, span(t, face)], target, 2 * t + h)

    def plane_copies(c):
        return [
            remote(
                part.at[c, span(lax.rem(low + step, inner), slab)],
                first_in.at[c, step - 1], "one", c, step - 1, dom=plane[step - 1],
            )
            for step in range(1, inner)
        ]

    def line_copies(c):
        return [
            remote(
                first_sum.at[c, span(lax.rem(high + step, outer), piece)],
                second_in.at[c, step - 1], "two", c, step - 1, dom=line[step - 1],
            )
            for step in range(1, outer)
        ]

    own_slab = span(low, slab)
    own_piece = pl.ds(pl.multiple_of(low * slab + high * piece, piece), piece)

    def line_back(c):
        spot = gathered.at[me, c, own_piece]
        return [remote(spot, spot, "three", c, s - 1, dom=line[s - 1]) for s in range(1, outer)]

    def plane_back(c):
        spot = gathered.at[me, c, own_slab]
        return [remote(spot, spot, "four", c, s - 1, dom=plane[s - 1]) for s in range(1, inner)]

    def band_back(c):
        spot = gathered.at[me, c]
        return remote(spot, spot, "five", c, band=partner)

    def emit(c, left, right):
        value = dot32(everyone[left], everyone[right], ((0,), (0,)))
        part[c] = (value * (1.0 / (own * domains))).astype(bf16)
        for copy in plane_copies(c):
            copy.start()

    for k in range(3):
        for h in range(2):
            advance(k, h)
            if k < 2:
                send_faces(k + 1, h)
                send_returned(k + 1, h)
            else:
                band_copy(h).start()
                if h == 0:
                    emit(0, 2 * me, 2 * me)
    emit(1, 2 * me, 2 * me + 1)
    emit(2, 2 * me + 1, 2 * me + 1)
    for h in range(2):
        band_copy(h).wait()
    for i in range(2):
        emit(3 + i, 2 * me + i, 2 * partner + i + me - 2 * i * me)

    for c in range(chunks):
        total = part[c, own_slab].astype(f32)
        for step, copy in enumerate(plane_copies(c)):
            copy.wait()
            total = total + first_in[c, step].astype(f32)
        first_sum[c] = total.astype(bf16)
        for copy in line_copies(c):
            copy.start()
    for c in range(chunks):
        total = first_sum[c, span(high, piece)].astype(f32)
        for step, copy in enumerate(line_copies(c)):
            copy.wait()
            total = total + second_in[c, step].astype(f32)
        gathered[me, c, own_piece] = total.astype(bf16)
        for copy in line_back(c):
            copy.start()
    for c in range(chunks):
        for copy in line_back(c):
            copy.wait()
        for copy in plane_back(c):
            copy.start()
    for c in range(chunks):
        for copy in plane_back(c):
            copy.wait()
        band_back(c).start()
    for c in range(chunks):
        band_back(c).wait()

    unit = (
        lax.broadcasted_iota(jnp.int32, (block, block), 0)
        == lax.broadcasted_iota(jnp.int32, (block, block), 1)
    ).astype(f32)
    trace = 0.0
    for q in range(2):
        for c in (0, 2):
            trace = trace + jnp.sum(gathered[q, c].astype(f32) * unit)
    mean_eigen = jnp.full((1, 1), trace, f32) / states
    inverse = 1.0 / mean_eigen
    scale_ref[...] = jnp.broadcast_to(lax.rsqrt(mean_eigen), scale_ref.shape)
    for q in range(2):
        for c, (i, j) in enumerate(upper_blocks(q)):
            value = gathered[q, c].astype(f32) * inverse
            if i == j:
                value = value - unit
            offset[i * block : (i + 1) * block, j * block : (j + 1) * block] = value.astype(bf16)
            if i != j:
                offset[j * block : (j + 1) * block, i * block : (i + 1) * block] = value.T.astype(bf16)

    mine = pl.ds(pl.multiple_of(me * width, 128), width)

    @pl.loop(0, states // block)
    def _(r):
        rows = span(r, block)
        value = dot32(offset[rows, :], offset[:, mine])
        second[rows, :] = value
        term[rows, :] = value.astype(bf16)

    @pl.loop(0, states // block)
    def _(r):
        rows = span(r, block)
        value = dot32(offset[rows, :], term[...])
        third[rows, :] = (value / 16.0 - second[rows, :] * (5.0 / 16.0)).astype(bf16)

    @pl.loop(0, states // block)
    def _(r):
        rows = span(r, block)
        tail = dot32(offset[rows, :], third[...])
        first = offset[rows, mine].astype(f32)
        change[rows, :] = (tail + 0.375 * second[rows, :] - 0.5 * first).astype(bf16)

    @pl.loop(0, own // face)
    def _(t):
        rows = span(t, face)
        value = jnp.concatenate([states_one[0, rows, :], states_one[1, rows, :]], axis=1)
        for q in range(4):
            value = value + dot32(everyone[q, rows, :], change[q * block : (q + 1) * block, :])
        for h in range(2):
            states_two[h, rows, :] = value[:, h * block : (h + 1) * block]
            out_copy(t, h).start()

    @pl.loop(0, own // face)
    def _(t):
        for h in range(2):
            out_copy(t, h).wait()


def fused(wavefunctions, mass_scale, cell_matrices, connectivity, face_index, domains):
    bf16, f32 = jnp.bfloat16, jnp.float32
    own, width = wavefunctions.shape
    face = face_index.shape[0]
    cells, nodes = connectivity.shape
    extent, share = own + face, (own + face) // 2
    states, block = 2 * width, width // 2
    inner, outer = split_domains(domains)
    slab = block // inner
    piece = slab // outer
    vmem = pl.BlockSpec(memory_space=pltpu.VMEM)
    hbm = pl.BlockSpec(memory_space=pl.ANY)
    dma = pltpu.SemaphoreType.DMA
    scratch = dict(
        matrix=pltpu.VMEM((extent, extent), bf16),
        b=pltpu.VMEM((cells * nodes, share), bf16),
        picks=pltpu.VMEM((nodes, share), bf16),
        picks_next=pltpu.VMEM((nodes, share), bf16),
        hits=pltpu.VMEM((face, cells * nodes), bf16),
        mass_all=pltpu.VMEM((own, 128), f32),
        face_column=pltpu.VMEM((face, 128), jnp.int32),
        face_of=pltpu.VMEM((face, own), bf16),
        face_in=pltpu.VMEM((own, face), bf16),
        scaled=pltpu.VMEM((2, own, block), bf16),
        sent=pltpu.VMEM((3, 2, 2 * face, block), bf16),
        returned_in=pltpu.VMEM((3, 2, face, block), bf16),
        faces_in=pltpu.VMEM((3, 2, face, block), bf16),
        corner_in=pltpu.VMEM((face, face), bf16),
        rests=pltpu.VMEM((2, extent, 128), bf16),
        rest_all=pltpu.VMEM((extent, 128), f32),
        lost=pltpu.VMEM((8, share), f32),
        corner_rest=pltpu.VMEM((face, 128), bf16),
        corner_rest_in=pltpu.VMEM((face, 128), bf16),
        added_low=pltpu.VMEM((face, block), bf16),
        states_one=pltpu.VMEM((2, own, block), f32),
        states_two=pltpu.VMEM((2, own, block), f32),
        everyone=pltpu.VMEM((4, own, block), bf16),
        part=pltpu.VMEM((5, block, block), bf16),
        first_in=pltpu.VMEM((5, inner - 1, slab, block), bf16),
        first_sum=pltpu.VMEM((5, slab, block), bf16),
        second_in=pltpu.VMEM((5, outer - 1, piece, block), bf16),
        gathered=pltpu.VMEM((2, 5, block, block), bf16),
        offset=pltpu.VMEM((states, states), bf16),
        second=pltpu.VMEM((states, width), f32),
        third=pltpu.VMEM((states, width), bf16),
        term=pltpu.VMEM((states, width), bf16),
        local_sem=dma((2 * own // face,)),
    )
    counts = dict(
        face=(3, 2), corner=(2,), matrix=(extent // face,), rest=(extent // face,), band=(2,),
        one=(5, inner - 1), two=(5, outer - 1), three=(5, outer - 1), four=(5, inner - 1), five=(5,),
    )
    counts["return"] = (3, 2)
    for name, shape in counts.items():
        scratch[name + "_send"] = dma(shape)
        scratch[name + "_recv"] = dma(shape)
    names = ("conn_ref", "a_ref", "mass_ref", "face_ref", "wave_ref", "out_ref", "scale_ref")
    turned, scale = pl.pallas_call(
        functools.partial(fused_kernel, inner, outer, names + tuple(scratch)),
        out_shape=(
            jax.ShapeDtypeStruct((own, width), f32),
            jax.ShapeDtypeStruct((1, width), f32),
        ),
        in_specs=[vmem] * 5,
        out_specs=(hbm, vmem),
        scratch_shapes=list(scratch.values()),
        compiler_params=pltpu.CompilerParams(
            vmem_limit_bytes=FUSED_LIMIT, collective_id=1, has_side_effects=True
        ),
        name="fused",
    )(connectivity, cell_matrices, mass_scale[None, :], face_index[None, :], wavefunctions)
    return turned * scale


def fits(own, width, face, cells, domains):
    return (
        lax.axis_size("band") == 2
        and min(split_domains(domains)) > 1
        and width % (32 * domains) == 0
        and width % 256 == 0
        and face % 128 == 0
        and own % face == 0
        and (own + face) % 256 == 0
        and cells % 2 == 0
    )


def passed_along(value, axis, steps):
    count = lax.axis_size(axis)
    initial, last = (max(0, -steps), min(count, count - steps))
    return lax.ppermute(value, axis, [(source, source + steps) for source in range(initial, last)])


def on_device(wavefunctions, mass_scale, cell_matrices, connectivity, face_index):
    bf16 = jnp.bfloat16
    own, band_width = wavefunctions.shape
    face = face_index.shape[0]
    domains = lax.axis_size("dom")
    states = band_width * lax.axis_size("band")
    if fits(own, band_width, face, connectivity.shape[0], domains):
        return fused(wavefunctions, mass_scale, cell_matrices, connectivity, face_index, domains)
    matrix, rest = domain_operator(cell_matrices, connectivity, own + face)
    face_of = (face_index[:, None] == lax.broadcasted_iota(jnp.int32, (face, own), 1)).astype(bf16)
    face_in = (face_index[None, :] == lax.broadcasted_iota(jnp.int32, (own, face), 0)).astype(bf16)
    outgoing = jnp.concatenate([matrix[own:, :own], face_of], axis=0)
    inner = matrix[:own, :own]
    edge = jnp.concatenate([matrix[:own, own:], face_in, face_in], axis=1)
    corner = jnp.concatenate([matrix[own:, own:], rest[own:].astype(bf16)], axis=1)
    corner = passed_along(corner, "dom", 1)
    corner, corner_rest = corner[:, :face], corner[:, face : face + 1].astype(jnp.float32)
    rest = rest[:own, :1]
    mass = mass_scale[:, None]

    def hamiltonian(vectors):
        scaled = (mass * vectors).astype(bf16)
        sent = dot32(outgoing, scaled).astype(bf16)
        returned = passed_along(sent[:face], "dom", 1)
        received = passed_along(sent[face:], "dom", -1)
        summed = dot32(inner, scaled) + rest * scaled.astype(jnp.float32)
        added = returned.astype(jnp.float32) + dot32(corner, sent[face:])
        added = added + corner_rest * sent[face:].astype(jnp.float32)
        high = added.astype(bf16)
        low = (added - lax.reduce_precision(added, 8, 7)).astype(bf16)
        summed = summed + dot32(edge, jnp.concatenate([received, high, low], axis=0))
        return mass * summed

    previous = wavefunctions.astype(jnp.float32)
    current = (hamiltonian(previous) - filter_center * previous) / filter_half
    for _ in range(2):
        following = 2.0 * (hamiltonian(current) - filter_center * current) / filter_half - previous
        previous, current = (current, following)
    rounded = current.astype(bf16)
    everyone = lax.all_gather(rounded, "band", axis=1, tiled=True)
    partial = dot32(everyone, rounded, ((0,), (0,))) / (own * domains)
    tile = lax.psum_scatter(partial.astype(bf16), "dom", scatter_dimension=0, tiled=True)
    columns = lax.all_gather(tile, "dom", axis=0, tiled=True)
    margin = lax.all_gather(columns, "band", axis=1, tiled=True).astype(jnp.float32)
    identity = (
        lax.broadcasted_iota(jnp.int32, (states, states), 0)
        == lax.broadcasted_iota(jnp.int32, (states, states), 1)
    ).astype(jnp.float32)
    mean_eigen = jnp.sum(margin * identity) / states
    offset = (margin / mean_eigen - identity).astype(bf16)
    start = lax.axis_index("band") * band_width
    first = lax.dynamic_slice_in_dim(columns.astype(jnp.float32), 0, states, 0) / mean_eigen
    first = first - lax.dynamic_slice_in_dim(identity, start, band_width, 1)
    second = dot32(offset, first.astype(bf16))
    third = dot32(offset, second.astype(bf16))
    tail = dot32(offset, (third / 16.0 - second * (5.0 / 16.0)).astype(bf16))
    change = tail + 0.375 * second - 0.5 * first
    turned = current + dot32(everyone, change.astype(bf16))
    return turned / jnp.sqrt(mean_eigen)


def solution(mesh):
    return jax.shard_map(
        on_device,
        mesh=mesh,
        in_specs=(P("dom", "band"), P("dom"), P("dom", None, None), P("dom", None), P("dom")),
        out_specs=P("dom", "band"),
        check_vma=False,
    )
```
